32 devices in a mesh: dp: 8 (over z, core), tensor: 4 (over y, x).
Axes of the slice: x: 2, y: 2, z: 4, core: 2. Of those that a mesh axis runs over, the one named last changes fastest.
Arguments:
- tokens_in: bfloat16 [1024, 8192], P(('dp', 'tensor')), may hold values from -6 to 6
- projector: bfloat16 [8192, 512], P('tensor'), may hold values from -0.0625 to 0.0625
- gate_pre: bfloat16 [1024, 15360], P('dp', 'tensor'), may hold values from -6 to 6
- up_pre: bfloat16 [1024, 15360], P('dp', 'tensor'), may hold values from -6 to 6
- hidden_grad: bfloat16 [1024, 15360], P('dp', 'tensor'), may hold values from -6 to 6
- moment_m: float32 [15360, 1024], P(('tensor', 'dp')), may hold values from -4 to 4
- moment_v: float32 [15360, 1024], P(('tensor', 'dp')), may hold values from 0.05 to 1
Outputs:
- m_next: float32 [15360, 1024], P(('tensor', 'dp'))
- v_next: float32 [15360, 1024], P(('tensor', 'dp'))
- direction: float32 [15360, 1024], P(('tensor', 'dp'))
The draws below stay inside these ranges and needn't reach their ends.
All inputs are finite; a program needn't handle non-finite values.
Results may differ from the reference program's by a relative error of at most 0.00098.
Values may be sent and summed in bfloat16 or wider, within the bound.
A program may use at most 64 MiB of HBM per device.

```python
import math
import jax
import jax.numpy as jnp
from jax import lax

D = 8192
FF = 15360
R = 512
TOK_GRP = 128
TOKENS = 1024


def spiked(drawn, own_key, source, target, shards_of, factor):
    def block_of(axis_at):
        return (jnp.arange(drawn.shape[axis_at]) // (drawn.shape[axis_at] // shards_of)).reshape((-1,) + (1,) * (drawn.ndim - 1 - axis_at))

    first = jax.random.permutation(own_key, shards_of)[block_of(target)]
    far = (block_of(target) + shards_of // 2) % shards_of
    return jnp.where((block_of(source) == first) | (block_of(source) == far), factor * drawn, drawn)


def level_of(rng, extent, pieces, low, high):
    factor_of, own = 1.0, jax.random.fold_in(rng, 6)
    for axis_at, blocks in pieces:
        heights = jnp.exp(jax.random.uniform(jax.random.fold_in(own, axis_at), (blocks,), jnp.float32, low / len(pieces), high / len(pieces)))
        factor_of = factor_of * jnp.repeat(heights, extent[axis_at] // blocks).reshape([-1 if axis == axis_at else 1 for axis in range(len(extent))])
    return factor_of


def centred(rng, shape, deviation, bound, cuts=(), kind=jnp.bfloat16):
    result = deviation * jax.random.normal(rng, shape, jnp.float32)
    if cuts:
        result = result * level_of(rng, shape, cuts, -0.22, 0.18)
    return jnp.clip(result, -bound, bound).astype(kind)


def bell_draw_with(stream_key, extent, scale, most, shards, heavy, dtype=jnp.bfloat16):
    entries = scale * jax.random.normal(stream_key, extent, jnp.float32)
    if shards:
        entries = entries * level_of(stream_key, extent, shards, -0.22, 0.18)
    return jnp.clip(spiked(entries, jax.random.fold_in(stream_key, 3), *heavy), -most, most).astype(dtype)


def setup_inputs(seed: int = 0) -> dict:
    splits = jax.random.split(jax.random.key(seed), 8)
    return {
        "tokens_in": centred(splits[0], (TOKENS, D), 1.0, 6.0, ((0, 32),)),
        "projector": centred(splits[1], (D, R), D ** -0.5, 0.0625, ((0, 4),)),
        "gate_pre": centred(splits[2], (TOKENS, FF), 1.0, 6.0, ((0, 8), (1, 4))),
        "up_pre": centred(splits[3], (TOKENS, FF), 1.0, 6.0, ((0, 8), (1, 4))),
        "hidden_grad": bell_draw_with(splits[4], (TOKENS, FF), 1.0, 6.0, ((0, 8), (1, 4)), (0, 1, 8, 2.0)),
        "moment_m": centred(splits[5], (FF, 2 * R), 0.5, 4.0, ((0, 32),), jnp.float32),
        "moment_v": jnp.clip(jnp.exp(math.log(1.0) - 2.9957323 * jax.random.uniform(splits[6], (FF, 2 * R), jnp.float32) ** level_of(splits[6], (FF, 2 * R), ((0, 32),), -0.2, 0.2)), 0.05, 1.0),
    }


def group_terms(gate_blk, up_blk, hgrad_blk, xp_blk):
    gate = gate_blk.astype(jnp.float32)
    upval = up_blk.astype(jnp.float32)
    hgrad = hgrad_blk.astype(jnp.float32)
    sig = jax.nn.sigmoid(gate)
    grad_gate = (hgrad * upval * sig * (1.0 + gate * (1.0 - sig))).astype(jnp.bfloat16)
    grad_up = (hgrad * gate * sig).astype(jnp.bfloat16)
    first = jnp.dot(grad_gate.T, xp_blk, preferred_element_type=jnp.float32)
    second = jnp.dot(grad_up.T, xp_blk, preferred_element_type=jnp.float32)
    return jnp.concatenate([first, second], axis=1)

def reference(tokens_in, projector, gate_pre, up_pre, hidden_grad, moment_m, moment_v):
    groups = gate_pre.shape[0] // TOK_GRP
    xp = jnp.dot(tokens_in, projector, preferred_element_type=jnp.float32).astype(jnp.bfloat16)
    width = gate_pre.shape[1]
    stacked = (gate_pre.reshape(groups, TOK_GRP, width), up_pre.reshape(groups, TOK_GRP, width), hidden_grad.reshape(groups, TOK_GRP, width), xp.reshape(groups, TOK_GRP, xp.shape[1]))

    def accumulate(total, blocks):
        return (total + group_terms(blocks[0], blocks[1], blocks[2], blocks[3]), None)
    start = jnp.zeros((width, 2 * xp.shape[1]), jnp.float32)
    total, unused = lax.scan(accumulate, start, stacked)
    proj = total * float(TOKENS) ** (-0.5)
    m_next = 0.9 * moment_m + 0.1 * proj
    v_next = 0.95 * moment_v + 0.05 * proj * proj
    direction = m_next / (jnp.sqrt(v_next) + 1e-08)
    return (m_next, v_next, direction)
```

```python
import functools

import jax
import jax.numpy as jnp
from jax import lax
from jax.experimental import pallas as pl
from jax.experimental.pallas import tpu as pltpu
from jax.sharding import PartitionSpec as P


MESH = pl.DeviceIdType.MESH
TAILS = 3
OUTER_EARLY = ((1, 2, 0), (1, 0, 0), (0, 0, 1))
OUTER = ((1, 3, 0), (1, 1, 0), (0, 1, 1), (1, 2, 1), (1, 0, 1), (1, 3, 1), (1, 1, 1))
INNER_EARLY = ((0, 2, 0), (1, 0, 0), (1, 1, 0))
EARLY_CUTS = ((0, 0),)
INNER = ((0, 3, 0), (0, 2, 1), (0, 3, 1))
OWN = ((1, 0, 1), (1, 1, 1))
def pieces(rows):
    cuts = [-(-rows * i // (16 * TAILS)) * 16 for i in range(TAILS)] + [rows]
    return list(zip(cuts, cuts[1:]))


def exchange_kernel(
    ndp, nt, tok_ref, prj_ref, gate_ref, up_ref, hg_ref, out_ref,
    acts, prj_v, cols, part, rs_buf, xp_all, grads, recv,
    load_sem, tok_send, tok_recv, rs_send, rs_recv,
    xp_send, xz_recv, xt_recv, xc_recv, g_send, g_recv, cut_recv, late,
):
    d = lax.axis_index("dp")
    t = lax.axis_index("tensor")
    nz = ndp // 2
    z, c = d // 2, d % 2
    sub = tok_ref.shape[0]
    grp = sub * nt
    dcol = tok_ref.shape[1] // nt
    rows = recv.shape[2]
    rank = prj_ref.shape[1]
    half = ndp // 2
    half_tiles = half * rows // 128
    cut = pieces(rows)

    own_half = d // half
    inner = (z + 1) // 2 % 2
    up = z % 2
    adj = z + 1 - 2 * up
    far = (nz - 1) * (1 - z // 2)
    opp = 2 - z // 2
    first = own_half * (1 - inner) + (1 - own_half) * inner
    second = 1 - first

    def dest_of(which, j):
        return which * half + up * j + (1 - up) * (half - 1 - j)

    head = -(-rows // 128)
    spans = ((first, 0, head), (first, head, half_tiles), (second, 0, half_tiles))
    loads, places = [], []
    for i, (which, start, stop) in enumerate(spans):
        low = which * half_tiles + up * start + (1 - up) * (half_tiles - stop)
        at = pl.ds(pl.multiple_of(low * 128, 128), (stop - start) * 128)
        places.append(at)
        for k, src in enumerate((gate_ref, up_ref, hg_ref)):
            loads.append(pltpu.make_async_copy(src.at[:, at], acts.at[k, :, at], load_sem.at[i]))
    load_prj = pltpu.make_async_copy(prj_ref, prj_v, load_sem.at[3])
    own_tok = pltpu.make_async_copy(
        tok_ref.at[:, pl.ds(pl.multiple_of(t * dcol, 128), dcol)],
        cols.at[pl.ds(pl.multiple_of(t * sub, 16), sub), :],
        tok_recv.at[0],
    )
    for load in loads[:3]:
        load.start()

    def drain(ref, sem):
        pltpu.make_async_copy(ref, ref, sem).wait()

    barrier = pltpu.get_barrier_semaphore()

    def greet(dp, tensor):
        pl.semaphore_signal(barrier, inc=1, device_id=(dp, tensor), device_id_type=MESH)

    @pl.when(z < nz - 1)
    def _():
        for k in range(1, ndp):
            greet((d + k) % ndp, t)

    @pl.when(z == nz - 1)
    def _():
        greet(d + 1 - 2 * c, t)

    for k in range(1, nt):
        greet(d, (t + k) % nt)

    for load in loads[3:]:
        load.start()
    load_prj.start()
    own_tok.start()

    def tok_copy(dest, src):
        return pltpu.make_async_remote_copy(
            src_ref=tok_ref.at[:, pl.ds(pl.multiple_of(dest * dcol, 128), dcol)],
            dst_ref=cols.at[pl.ds(pl.multiple_of(src * sub, 16), sub), :],
            send_sem=tok_send.at[0],
            recv_sem=tok_recv.at[0],
            device_id=(d, dest),
            device_id_type=MESH,
        )

    def tile(i, carry):
        at = pl.ds(pl.multiple_of(i * 128, 128), 128)
        gate = acts[0, :, at].astype(jnp.float32)
        upval = acts[1, :, at].astype(jnp.float32)
        hgrad = acts[2, :, at].astype(jnp.float32)
        sig = jax.nn.sigmoid(gate)
        grad_gate = hgrad * upval * sig * (1.0 + gate * (1.0 - sig))
        grad_up = hgrad * gate * sig
        grads[0, at, :] = grad_gate.astype(jnp.bfloat16).T
        grads[1, at, :] = grad_up.astype(jnp.bfloat16).T
        return carry

    def tiles_of(which, start, stop):
        low = which * half_tiles + up * start + (1 - up) * (half_tiles - stop)
        lax.fori_loop(low, low + stop - start, tile, 0)

    def block_of(dest, side):
        return grads.at[side, pl.ds(pl.multiple_of(dest * rows, 16), rows), :]

    def grad_copy(dest, src, side):
        return pltpu.make_async_remote_copy(
            src_ref=block_of(dest, side),
            dst_ref=recv.at[src, side],
            send_sem=g_send.at[0],
            recv_sem=g_recv.at[src // 2 * 2 + side],
            device_id=(dest, t),
            device_id_type=MESH,
        )

    def cut_copy(dest, src, p):
        start, stop = cut[p]
        at = pl.ds(pl.multiple_of(dest * rows + start, 16), stop - start)
        return pltpu.make_async_remote_copy(
            src_ref=grads.at[1, at, :],
            dst_ref=recv.at[src, 1, start:stop, :],
            send_sem=g_send.at[0],
            recv_sem=cut_recv.at[p],
            device_id=(dest, t),
            device_id_type=MESH,
        )

    def own_grad(side):
        return pltpu.make_async_copy(block_of(d, side), recv.at[d, side], g_recv.at[2 * z + side])

    def send_near(dest, side):
        @pl.when(dest != d)
        def _():
            grad_copy(dest, d, side).start()

        @pl.when(dest == d)
        def _():
            own_grad(side).start()

    def send(which, j, side):
        grad_copy(dest_of(which, j), d, side).start()

    def send_all(plan):
        for part_of, j, side in plan:
            send((first, second)[part_of], j, side)

    def send_cuts(plan):
        for p, j in plan:
            cut_copy(dest_of(first, j), d, p).start()

    def need(j):
        return -(-((j + 1) * rows) // 128)

    drain(acts.at[:, :, places[0]], load_sem.at[0])
    tiles_of(first, 0, head)
    pl.semaphore_wait(barrier, nt - 1 + jnp.where(z == nz - 1, ndp - 1, ndp - 3))
    send(first, 0, 0)
    for k in range(1, nt):
        tok_copy((t + k) % nt, t).start()

    @pl.when(z == nz - 1)
    def _():
        for k in range(ndp - 2):
            pl.semaphore_signal(late, inc=1, device_id=(k, t), device_id_type=MESH)

    drain(acts.at[:, :, places[1]], load_sem.at[1])
    tiles_of(first, head, need(1))
    send(first, 1, 0)
    tiles_of(first, need(1), half_tiles)
    drain(acts.at[:, :, places[2]], load_sem.at[2])
    tiles_of(second, 0, half_tiles)

    @pl.when(z < nz - 1)
    def _():
        pl.semaphore_wait(late, 2)

    @pl.when(inner == 0)
    def _():
        send_all(OUTER_EARLY)

    @pl.when(inner == 1)
    def _():
        send_all(INNER_EARLY)
        send_cuts(EARLY_CUTS)

    for j in (2, 3):
        for side in (0, 1):
            send_near(dest_of(own_half, j), side)

    load_prj.wait()
    drain(cols, tok_recv.at[0])
    part[...] = jnp.dot(cols[...], prj_v[...], preferred_element_type=jnp.float32)

    def rs_copy(dest, src):
        return pltpu.make_async_remote_copy(
            src_ref=part.at[pl.ds(pl.multiple_of(dest * sub, 16), sub), :],
            dst_ref=rs_buf.at[src],
            send_sem=rs_send.at[0],
            recv_sem=rs_recv.at[0],
            device_id=(d, dest),
            device_id_type=MESH,
        )

    for k in range(1, nt):
        rs_copy((t + k) % nt, t).start()
    rs_buf[t] = part[pl.ds(pl.multiple_of(t * sub, 16), sub), :]
    drain(rs_buf.at[: nt - 1], rs_recv.at[0])
    total = rs_buf[0]
    for k in range(1, nt):
        total = total + rs_buf[k]

    def piece(dd, tt):
        return xp_all.at[pl.ds(pl.multiple_of(dd * grp + tt * sub, 16), sub), :]

    xp_all[pl.ds(pl.multiple_of(d * grp + t * sub, 16), sub), :] = total.astype(jnp.bfloat16)

    def piece_copy(dd, tt, recv_sem, dest):
        return pltpu.make_async_remote_copy(
            src_ref=piece(dd, tt),
            dst_ref=piece(dd, tt),
            send_sem=xp_send.at[0],
            recv_sem=recv_sem,
            device_id=dest,
            device_id_type=MESH,
        )

    def along_z(zz, dest):
        piece_copy(zz * 2 + c, t, xz_recv.at[zz], (dest * 2 + c, t)).start()

    along_z(z, opp)
    along_z(z, adj)

    @pl.when(inner == 0)
    def _():
        send_all(OUTER)

    @pl.when(inner == 1)
    def _():
        send_all(INNER)
        send_cuts([(p, j) for p in range(TAILS) for j in (0, 1) if (p, j) not in EARLY_CUTS])

    order = [z, adj, far, opp]

    for k, zz in enumerate(order):
        dd = zz * 2 + c
        if k:
            drain(piece(dd, t), xz_recv.at[zz])
        if k > 1:
            pl.when(inner == 1)(functools.partial(along_z, zz, adj))
        for kt in range(1, nt):
            piece_copy(dd, t, xt_recv.at[zz], (d, (t + kt) % nt)).start()

    @pl.when(inner == 1)
    def _():
        send_all(OWN)

    partner = d + 1 - 2 * c

    def core_copy(zz, parity):
        group = xp_all.at[pl.ds(pl.multiple_of((zz * 2 + parity) * grp, 128), grp), :]
        return pltpu.make_async_remote_copy(
            src_ref=group,
            dst_ref=group,
            send_sem=xp_send.at[0],
            recv_sem=xc_recv.at[zz],
            device_id=(partner, t),
            device_id_type=MESH,
        )

    for zz in order:
        drain(xp_all.at[: (nt - 1) * sub, :], xt_recv.at[zz])
        core_copy(zz, c).start()

    def add_term(k, zz, side, low, count):
        at = pl.ds(low, count)
        xp = xp_all[pl.ds(pl.multiple_of(zz * 2 * grp, 128), 2 * grp), :]
        lhs = jnp.concatenate([recv[zz * 2, side, at, :], recv[zz * 2 + 1, side, at, :]], axis=1)
        term = jnp.dot(lhs, xp, preferred_element_type=jnp.float32)
        cols_at = slice(side * rank, (side + 1) * rank)
        if k == 0:
            out_ref[at, cols_at] = term
        else:
            out_ref[at, cols_at] += term

    def take(k, zz, side):
        drain(recv.at[pl.ds(zz * 2, 2), side], g_recv.at[2 * zz + side])
        add_term(k, zz, side, 0, rows)

    for k in (0, 1):
        core_copy(order[k], 1 - c).wait_recv()
        for side in (0, 1):
            take(k, order[k], side)
    core_copy(far, 1 - c).wait_recv()
    core_copy(opp, 1 - c).wait_recv()
    drain(cols.at[: (nt - 1) * sub, :], tok_send.at[0])
    drain(rs_buf.at[: nt - 1], rs_send.at[0])
    moved = (nt - 1) * nz + nt * nz + 2
    pl.when(inner == 0)(lambda: drain(xp_all.at[: moved * sub, :], xp_send.at[0]))
    pl.when(inner == 1)(lambda: drain(xp_all.at[: (moved + 2) * sub, :], xp_send.at[0]))
    take(3, opp, 0)
    take(2, far, 0)
    take(2, far, 1)

    @pl.when(inner == 0)
    def _():
        take(3, opp, 1)

    @pl.when(inner == 1)
    def _():
        for p, (start, stop) in enumerate(cut):
            drain(recv.at[pl.ds(opp * 2, 2), 1, start:stop, :], cut_recv.at[p])
            add_term(3, opp, 1, start, stop - start)

    drain(recv.at[: ndp - 1], g_send.at[0])


def exchange(ndp, nt, tokens_in, projector, gate_pre, up_pre, hidden_grad):
    sub, width = tokens_in.shape
    depth, rank = projector.shape
    grp, cols = gate_pre.shape
    rows = cols // ndp
    dma = pltpu.SemaphoreType.DMA
    bf, f32 = jnp.bfloat16, jnp.float32
    nz = ndp // 2
    operands = (tokens_in, projector, gate_pre, up_pre, hidden_grad)
    flops = 2 * grp * depth * rank + 4 * rows * grp * ndp * rank
    return pl.pallas_call(
        functools.partial(exchange_kernel, ndp, nt),
        out_shape=jax.ShapeDtypeStruct((rows, 2 * rank), f32),
        in_specs=[pl.BlockSpec(memory_space=pltpu.HBM)] * 5,
        out_specs=pl.BlockSpec(memory_space=pltpu.VMEM),
        scratch_shapes=[
            pltpu.VMEM((3, grp, cols), bf),
            pltpu.VMEM((depth, rank), bf),
            pltpu.VMEM((grp, depth), bf),
            pltpu.VMEM((grp, rank), f32),
            pltpu.VMEM((nt, sub, rank), f32),
            pltpu.VMEM((grp * ndp, rank), bf),
            pltpu.VMEM((2, cols, grp), bf),
            pltpu.VMEM((ndp, 2, rows, grp), bf),
            dma((4,)),
            dma((1,)),
            dma((1,)),
            dma((1,)),
            dma((1,)),
            dma((1,)),
            dma((nz,)),
            dma((nz,)),
            dma((nz,)),
            dma((1,)),
            dma((2 * nz,)),
            dma((TAILS,)),
            pltpu.SemaphoreType.REGULAR,
        ],
        compiler_params=pltpu.CompilerParams(
            collective_id=0, has_side_effects=True, vmem_limit_bytes=32 * 1024 * 1024
        ),
        cost_estimate=pl.CostEstimate(
            flops=flops, bytes_accessed=8 * grp * cols, transcendentals=grp * cols
        ),
    )(*[pltpu.with_memory_space_constraint(x, pltpu.HBM) for x in operands])


def fits(ndp, nt, tokens_in, projector, gate_pre):
    sub, width = tokens_in.shape
    grp, cols = gate_pre.shape
    return (
        ndp == 8
        and nt >= 2
        and grp == 128
        and sub * nt == grp
        and sub % 16 == 0
        and cols % ndp == 0
        and (cols // ndp) % 16 == 0
        and cols // ndp >= 256
        and cols % 256 == 0
        and width % (128 * nt) == 0
        and projector.shape[0] == width // nt
        and projector.shape[1] % 128 == 0
        and cols <= 8192
        and projector.size <= 2**21
        and grp * ndp <= 4096
    )


def finish(summed, total_tokens, moment_m, moment_v):
    proj = summed * float(total_tokens) ** (-0.5)
    m_next = 0.9 * moment_m + 0.1 * proj
    v_next = 0.95 * moment_v + 0.05 * proj * proj
    direction = m_next / (jnp.sqrt(v_next) + 1e-08)
    return (m_next, v_next, direction)


def finish_kernel(total_tokens, steps, sum_ref, m_ref, v_ref, *refs):
    outs, bufs, sem = refs[:3], refs[3:6], refs[6]
    rows = sum_ref.shape[0] // steps
    for i in range(steps):
        at = slice(i * rows, (i + 1) * rows)
        values = finish(sum_ref[at, :], total_tokens, m_ref[at, :], v_ref[at, :])
        for k in range(3):
            bufs[k][at, :] = values[k]
            copy = pltpu.make_async_copy(
                bufs[k].at[at, :], outs[k].at[at, :], sem.at[k]
            )
            copy.start()
    for k in range(3):
        pltpu.make_async_copy(bufs[k], outs[k], sem.at[k]).wait()


def finish_call(summed, total_tokens, moment_m, moment_v):
    steps = 6
    shape = jax.ShapeDtypeStruct(summed.shape, jnp.float32)
    return pl.pallas_call(
        functools.partial(finish_kernel, total_tokens, steps),
        out_shape=(shape,) * 3,
        in_specs=[pl.BlockSpec(memory_space=pltpu.VMEM)] * 3,
        out_specs=[pl.BlockSpec(memory_space=pltpu.HBM)] * 3,
        scratch_shapes=[pltpu.VMEM(summed.shape, jnp.float32)] * 3
        + [pltpu.SemaphoreType.DMA((3,))],
        compiler_params=pltpu.CompilerParams(vmem_limit_bytes=16 * 1024 * 1024),
    )(summed, moment_m, moment_v)


def local(tokens_in, projector, gate_pre, up_pre, hidden_grad, moment_m, moment_v):
    ndp, nt = lax.axis_size("dp"), lax.axis_size("tensor")
    if fits(ndp, nt, tokens_in, projector, gate_pre):
        summed = exchange(ndp, nt, tokens_in, projector, gate_pre, up_pre, hidden_grad)
        return tuple(finish_call(summed, gate_pre.shape[0] * ndp, moment_m, moment_v))
    gate = gate_pre.astype(jnp.float32)
    hgrad = hidden_grad.astype(jnp.float32)
    sig = jax.nn.sigmoid(gate)
    upval = up_pre.astype(jnp.float32)
    grad_gate = (hgrad * upval * sig * (1.0 + gate * (1.0 - sig))).astype(jnp.bfloat16)
    grad_up = (hgrad * gate * sig).astype(jnp.bfloat16)
    grads = jnp.stack([grad_gate, grad_up])
    grads = lax.all_to_all(grads, "dp", split_axis=2, concat_axis=1, tiled=True)
    columns = lax.all_to_all(tokens_in, "tensor", split_axis=1, concat_axis=0, tiled=True)
    partial_xp = jnp.dot(columns, projector, preferred_element_type=jnp.float32)
    own_rows = lax.psum_scatter(partial_xp, "tensor", scatter_dimension=0, tiled=True).astype(
        jnp.bfloat16
    )
    xp = lax.all_gather(own_rows, ("dp", "tensor"), axis=0, tiled=True)
    contract = (((0,), (0,)), ((), ()))
    halves = [
        lax.dot_general(grads[k], xp, contract, preferred_element_type=jnp.float32) for k in (0, 1)
    ]
    summed = jnp.concatenate(halves, axis=1)
    return finish(summed, xp.shape[0], moment_m, moment_v)


def solution(mesh):
    return jax.shard_map(
        local,
        mesh=mesh,
        in_specs=(
            P(("dp", "tensor"), None),
            P("tensor", None),
            P("dp", "tensor"),
            P("dp", "tensor"),
            P("dp", "tensor"),
            P(("tensor", "dp"), None),
            P(("tensor", "dp"), None),
        ),
        out_specs=(P(("tensor", "dp"), None), P(("tensor", "dp"), None), P(("tensor", "dp"), None)),
        check_vma=False,
    )
```

```python
import functools

import jax
import jax.numpy as jnp
from jax import lax
from jax.experimental import pallas as pl
from jax.experimental.pallas import tpu as pltpu
from jax.sharding import PartitionSpec as P


MESH = pl.DeviceIdType.MESH
TAILS = 3
OUTER_EARLY = (
    ((1, 2, 0), (1, 0, 0), (0, 0, 1)),
    ((0, 0, 1), (1, 0, 0), (1, 2, 0)),
)
OUTER = (
    ((1, 3, 0), (1, 1, 0), (0, 1, 1), (1, 2, 1), (1, 0, 1), (1, 3, 1), (1, 1, 1)),
    ((0, 1, 1), (1, 1, 0), (1, 3, 0), (1, 0, 1), (1, 2, 1), (1, 1, 1), (1, 3, 1)),
)
INNER_EARLY = (
    ((0, 2, 0), (1, 0, 0), (1, 1, 0), 0),
    ((0, 3, 0), (1, 0, 0), (1, 1, 0), 0),
)
INNER = (
    ((0, 3, 0), (1, 0, 1), (0, 2, 1), (0, 3, 1), 1, 2, 3, 4, 5),
    ((0, 2, 0), (1, 0, 1), (0, 3, 1), (0, 2, 1), 1, 2, 3, 4, 5),
)
LATER = ((1, 1, 1),)
def pieces(rows):
    cuts = [-(-rows * i // (16 * TAILS)) * 16 for i in range(TAILS)] + [rows]
    return list(zip(cuts, cuts[1:]))


def exchange_kernel(
    ndp, nt, tok_ref, prj_ref, gate_ref, up_ref, hg_ref, out_ref,
    acts, prj_v, cols, part, rs_buf, xp_all, grads, recv,
    load_sem, tok_send, tok_recv, rs_send, rs_recv,
    xp_send, xz_recv, xt_recv, xc_recv, g_send, g_recv, cut_recv, near, late,
):
    d = lax.axis_index("dp")
    t = lax.axis_index("tensor")
    nz = ndp // 2
    z, c = d // 2, d % 2
    sub = tok_ref.shape[0]
    grp = sub * nt
    dcol = tok_ref.shape[1] // nt
    rows = recv.shape[2]
    rank = prj_ref.shape[1]
    half = ndp // 2
    half_tiles = half * rows // 128
    cut = pieces(rows)

    own_half = d // half
    inner = (z + 1) // 2 % 2
    up = z % 2
    adj = z + 1 - 2 * up
    far = (nz - 1) * (1 - z // 2)
    opp = 2 - z // 2
    first = own_half * (1 - inner) + (1 - own_half) * inner
    second = 1 - first

    def dest_of(which, j):
        return which * half + up * j + (1 - up) * (half - 1 - j)

    head = -(-rows // 128)
    spans = ((first, 0, 1), (first, 1, half_tiles), (second, 0, half_tiles))
    loads, places = [], []
    for i, (which, start, stop) in enumerate(spans):
        low = which * half_tiles + up * start + (1 - up) * (half_tiles - stop)
        at = pl.ds(pl.multiple_of(low * 128, 128), (stop - start) * 128)
        places.append(at)
        for k, src in enumerate((gate_ref, up_ref, hg_ref)):
            loads.append(pltpu.make_async_copy(src.at[:, at], acts.at[k, :, at], load_sem.at[i]))
    load_prj = pltpu.make_async_copy(prj_ref, prj_v, load_sem.at[3])
    own_tok = pltpu.make_async_copy(
        tok_ref.at[:, pl.ds(pl.multiple_of(t * dcol, 128), dcol)],
        cols.at[pl.ds(pl.multiple_of(t * sub, 16), sub), :],
        tok_recv.at[0],
    )
    for load in loads[:3]:
        load.start()

    def drain(ref, sem):
        pltpu.make_async_copy(ref, ref, sem).wait()

    barrier = pltpu.get_barrier_semaphore()

    def greet(dp, tensor):
        pl.semaphore_signal(barrier, inc=1, device_id=(dp, tensor), device_id_type=MESH)

    @pl.when(z < nz - 1)
    def _():
        for k in range(1, ndp):
            greet((d + k) % ndp, t)

    @pl.when(z == nz - 1)
    def _():
        greet(d + 1 - 2 * c, t)

    host = inner * adj + (1 - inner) * z
    for k in range(1, nt):
        greet(host * 2 + c, (t + k) % nt)

    for load in loads[3:]:
        load.start()
    load_prj.start()
    own_tok.start()

    def tok_copy(dest, src):
        return pltpu.make_async_remote_copy(
            src_ref=tok_ref.at[:, pl.ds(pl.multiple_of(dest * dcol, 128), dcol)],
            dst_ref=cols.at[pl.ds(pl.multiple_of(src * sub, 16), sub), :],
            send_sem=tok_send.at[0],
            recv_sem=tok_recv.at[0],
            device_id=(d, dest),
            device_id_type=MESH,
        )

    def tile(i, carry):
        at = pl.ds(pl.multiple_of(i * 128, 128), 128)
        gate = acts[0, :, at].astype(jnp.float32)
        upval = acts[1, :, at].astype(jnp.float32)
        hgrad = acts[2, :, at].astype(jnp.float32)
        sig = jax.nn.sigmoid(gate)
        grad_gate = hgrad * upval * sig * (1.0 + gate * (1.0 - sig))
        grad_up = hgrad * gate * sig
        grads[0, at, :] = grad_gate.astype(jnp.bfloat16).T
        grads[1, at, :] = grad_up.astype(jnp.bfloat16).T
        return carry

    def tiles_of(which, start, stop):
        low = which * half_tiles + up * start + (1 - up) * (half_tiles - stop)
        lax.fori_loop(low, low + stop - start, tile, 0)

    def block_of(dest, side):
        return grads.at[side, pl.ds(pl.multiple_of(dest * rows, 16), rows), :]

    def grad_copy(dest, src, side):
        return pltpu.make_async_remote_copy(
            src_ref=block_of(dest, side),
            dst_ref=recv.at[src, side],
            send_sem=g_send.at[0],
            recv_sem=g_recv.at[src // 2 * 2 + side],
            device_id=(dest, t),
            device_id_type=MESH,
        )

    def cut_copy(dest, src, p):
        start, stop = cut[p]
        at = pl.ds(pl.multiple_of(dest * rows + start, 16), stop - start)
        return pltpu.make_async_remote_copy(
            src_ref=grads.at[1, at, :],
            dst_ref=recv.at[src, 1, start:stop, :],
            send_sem=g_send.at[0],
            recv_sem=cut_recv.at[p],
            device_id=(dest, t),
            device_id_type=MESH,
        )

    def own_grad(side):
        return pltpu.make_async_copy(block_of(d, side), recv.at[d, side], g_recv.at[2 * z + side])

    def send_near(dest, side):
        @pl.when(dest != d)
        def _():
            grad_copy(dest, d, side).start()

        @pl.when(dest == d)
        def _():
            own_grad(side).start()

    def send(which, j, side):
        grad_copy(dest_of(which, j), d, side).start()

    def send_all(kind, plans):
        for core, plan in enumerate(plans):

            @pl.when((inner == kind) & (c == core))
            def _():
                for item in plan:
                    if isinstance(item, int):
                        cut_copy(dest_of(first, item % 2), d, item // 2).start()
                    else:
                        send((first, second)[item[0]], *item[1:])

    def need(j):
        return -(-((j + 1) * rows) // 128)

    drain(acts.at[:, :, places[0]], load_sem.at[0])
    tiles_of(first, 0, 1)
    known = jnp.where(z == nz - 1, ndp - 1, ndp - 3)
    pl.semaphore_wait(barrier, known + (1 - inner) * 2 * (nt - 1))

    def part_send(start, stop):
        low = dest_of(first, 0) * rows + up * start + (1 - up) * (rows - stop)
        at = pl.ds(pl.multiple_of(low, 16), stop - start)
        back = up * start + (1 - up) * (rows - stop)
        pltpu.make_async_remote_copy(
            src_ref=grads.at[0, at, :],
            dst_ref=recv.at[d, 0, pl.ds(pl.multiple_of(back, 16), stop - start), :],
            send_sem=g_send.at[0],
            recv_sem=g_recv.at[2 * z],
            device_id=(dest_of(first, 0), t),
            device_id_type=MESH,
        ).start()

    def send_tokens():
        for k in range(1, nt):
            tok_copy((t + k) % nt, t).start()

    part_send(0, 128)

    @pl.when(inner == 0)
    def _():
        pl.semaphore_signal(near, inc=1, device_id=(adj * 2 + c, t), device_id_type=MESH)
        send_tokens()

    @pl.when(z == nz - 1)
    def _():
        for k in range(ndp - 2):
            pl.semaphore_signal(late, inc=1, device_id=(k, t), device_id_type=MESH)

    drain(acts.at[:, :, places[1]], load_sem.at[1])
    tiles_of(first, 1, head)
    part_send(128, rows)
    tiles_of(first, head, need(1))
    send(first, 1, 0)
    tiles_of(first, need(1), half_tiles)

    @pl.when(inner == 1)
    def _():
        pl.semaphore_wait(near, 1)
        send_tokens()

    drain(acts.at[:, :, places[2]], load_sem.at[2])
    tiles_of(second, 0, half_tiles)

    @pl.when(z < nz - 1)
    def _():
        pl.semaphore_wait(late, 2)

    send_all(0, OUTER_EARLY)
    send_all(1, INNER_EARLY)

    for j in (2, 3):
        for side in (0, 1):
            send_near(dest_of(own_half, j), side)

    load_prj.wait()
    drain(cols, tok_recv.at[0])
    part[...] = jnp.dot(cols[...], prj_v[...], preferred_element_type=jnp.float32)

    def rs_copy(dest, src):
        return pltpu.make_async_remote_copy(
            src_ref=part.at[pl.ds(pl.multiple_of(dest * sub, 16), sub), :],
            dst_ref=rs_buf.at[src],
            send_sem=rs_send.at[0],
            recv_sem=rs_recv.at[0],
            device_id=(d, dest),
            device_id_type=MESH,
        )

    for k in range(1, nt):
        rs_copy((t + k) % nt, t).start()
    rs_buf[t] = part[pl.ds(pl.multiple_of(t * sub, 16), sub), :]
    drain(rs_buf.at[: nt - 1], rs_recv.at[0])
    total = rs_buf[0]
    for k in range(1, nt):
        total = total + rs_buf[k]

    def piece(dd, tt):
        return xp_all.at[pl.ds(pl.multiple_of(dd * grp + tt * sub, 16), sub), :]

    xp_all[pl.ds(pl.multiple_of(d * grp + t * sub, 16), sub), :] = total.astype(jnp.bfloat16)

    def piece_copy(dd, tt, recv_sem, dest):
        return pltpu.make_async_remote_copy(
            src_ref=piece(dd, tt),
            dst_ref=piece(dd, tt),
            send_sem=xp_send.at[0],
            recv_sem=recv_sem,
            device_id=dest,
            device_id_type=MESH,
        )

    def along_z(zz, dest):
        piece_copy(zz * 2 + c, t, xz_recv.at[zz], (dest * 2 + c, t)).start()

    along_z(z, opp)
    along_z(z, adj)

    send_all(0, OUTER)
    send_all(1, INNER)

    order = [z, adj, far, opp]

    for k, zz in enumerate(order):
        dd = zz * 2 + c
        if k:
            drain(piece(dd, t), xz_recv.at[zz])
        if k > 1:
            pl.when(inner == 1)(functools.partial(along_z, zz, adj))
        for kt in range(1, nt):
            piece_copy(dd, t, xt_recv.at[zz], (d, (t + kt) % nt)).start()

    send_all(1, (LATER, LATER))

    partner = d + 1 - 2 * c

    def core_copy(zz, parity):
        group = xp_all.at[pl.ds(pl.multiple_of((zz * 2 + parity) * grp, 128), grp), :]
        return pltpu.make_async_remote_copy(
            src_ref=group,
            dst_ref=group,
            send_sem=xp_send.at[0],
            recv_sem=xc_recv.at[zz],
            device_id=(partner, t),
            device_id_type=MESH,
        )

    for zz in order:
        drain(xp_all.at[: (nt - 1) * sub, :], xt_recv.at[zz])
        core_copy(zz, c).start()

    def add_term(k, zz, side, low, count):
        at = pl.ds(low, count)
        xp = xp_all[pl.ds(pl.multiple_of(zz * 2 * grp, 128), 2 * grp), :]
        lhs = jnp.concatenate([recv[zz * 2, side, at, :], recv[zz * 2 + 1, side, at, :]], axis=1)
        term = jnp.dot(lhs, xp, preferred_element_type=jnp.float32)
        cols_at = slice(side * rank, (side + 1) * rank)
        if k == 0:
            out_ref[at, cols_at] = term
        else:
            out_ref[at, cols_at] += term

    def take(k, zz, side):
        drain(recv.at[pl.ds(zz * 2, 2), side], g_recv.at[2 * zz + side])
        add_term(k, zz, side, 0, rows)

    for k in (0, 1):
        core_copy(order[k], 1 - c).wait_recv()
        for side in (0, 1):
            take(k, order[k], side)
    core_copy(far, 1 - c).wait_recv()
    core_copy(opp, 1 - c).wait_recv()
    drain(cols.at[: (nt - 1) * sub, :], tok_send.at[0])
    drain(rs_buf.at[: nt - 1], rs_send.at[0])
    moved = (nt - 1) * nz + nt * nz + 2
    pl.when(inner == 0)(lambda: drain(xp_all.at[: moved * sub, :], xp_send.at[0]))
    pl.when(inner == 1)(lambda: drain(xp_all.at[: (moved + 2) * sub, :], xp_send.at[0]))
    take(3, opp, 0)
    take(2, far, 0)
    take(2, far, 1)

    @pl.when(inner == 0)
    def _():
        take(3, opp, 1)

    @pl.when(inner == 1)
    def _():
        for p, (start, stop) in enumerate(cut):
            drain(recv.at[pl.ds(opp * 2, 2), 1, start:stop, :], cut_recv.at[p])
            add_term(3, opp, 1, start, stop - start)

    drain(recv.at[: ndp - 1], g_send.at[0])


def exchange(ndp, nt, tokens_in, projector, gate_pre, up_pre, hidden_grad):
    sub, width = tokens_in.shape
    depth, rank = projector.shape
    grp, cols = gate_pre.shape
    rows = cols // ndp
    dma = pltpu.SemaphoreType.DMA
    bf, f32 = jnp.bfloat16, jnp.float32
    nz = ndp // 2
    operands = (tokens_in, projector, gate_pre, up_pre, hidden_grad)
    flops = 2 * grp * depth * rank + 4 * rows * grp * ndp * rank
    return pl.pallas_call(
        functools.partial(exchange_kernel, ndp, nt),
        out_shape=jax.ShapeDtypeStruct((rows, 2 * rank), f32),
        in_specs=[pl.BlockSpec(memory_space=pltpu.HBM)] * 5,
        out_specs=pl.BlockSpec(memory_space=pltpu.VMEM),
        scratch_shapes=[
            pltpu.VMEM((3, grp, cols), bf),
            pltpu.VMEM((depth, rank), bf),
            pltpu.VMEM((grp, depth), bf),
            pltpu.VMEM((grp, rank), f32),
            pltpu.VMEM((nt, sub, rank), f32),
            pltpu.VMEM((grp * ndp, rank), bf),
            pltpu.VMEM((2, cols, grp), bf),
            pltpu.VMEM((ndp, 2, rows, grp), bf),
            dma((4,)),
            dma((1,)),
            dma((1,)),
            dma((1,)),
            dma((1,)),
            dma((1,)),
            dma((nz,)),
            dma((nz,)),
            dma((nz,)),
            dma((1,)),
            dma((2 * nz,)),
            dma((TAILS,)),
            pltpu.SemaphoreType.REGULAR,
            pltpu.SemaphoreType.REGULAR,
        ],
        compiler_params=pltpu.CompilerParams(
            collective_id=0, has_side_effects=True, vmem_limit_bytes=32 * 1024 * 1024
        ),
        cost_estimate=pl.CostEstimate(
            flops=flops, bytes_accessed=8 * grp * cols, transcendentals=grp * cols
        ),
    )(*[pltpu.with_memory_space_constraint(x, pltpu.HBM) for x in operands])


def fits(ndp, nt, tokens_in, projector, gate_pre):
    sub, width = tokens_in.shape
    grp, cols = gate_pre.shape
    return (
        ndp == 8
        and nt >= 2
        and grp == 128
        and sub * nt == grp
        and sub % 16 == 0
        and cols % ndp == 0
        and (cols // ndp) % 16 == 0
        and cols // ndp >= 256
        and cols % 256 == 0
        and width % (128 * nt) == 0
        and projector.shape[0] == width // nt
        and projector.shape[1] % 128 == 0
        and cols <= 8192
        and projector.size <= 2**21
        and grp * ndp <= 4096
    )


def finish(summed, total_tokens, moment_m, moment_v):
    proj = summed * float(total_tokens) ** (-0.5)
    m_next = 0.9 * moment_m + 0.1 * proj
    v_next = 0.95 * moment_v + 0.05 * proj * proj
    direction = m_next / (jnp.sqrt(v_next) + 1e-08)
    return (m_next, v_next, direction)


def finish_kernel(total_tokens, steps, sum_ref, m_ref, v_ref, *refs):
    outs, bufs, sem = refs[:3], refs[3:6], refs[6]
    rows = sum_ref.shape[0] // steps
    for i in range(steps):
        at = slice(i * rows, (i + 1) * rows)
        values = finish(sum_ref[at, :], total_tokens, m_ref[at, :], v_ref[at, :])
        for k in range(3):
            bufs[k][at, :] = values[k]
            copy = pltpu.make_async_copy(
                bufs[k].at[at, :], outs[k].at[at, :], sem.at[k]
            )
            copy.start()
    for k in range(3):
        pltpu.make_async_copy(bufs[k], outs[k], sem.at[k]).wait()


def finish_call(summed, total_tokens, moment_m, moment_v):
    steps = 6
    shape = jax.ShapeDtypeStruct(summed.shape, jnp.float32)
    return pl.pallas_call(
        functools.partial(finish_kernel, total_tokens, steps),
        out_shape=(shape,) * 3,
        in_specs=[pl.BlockSpec(memory_space=pltpu.VMEM)] * 3,
        out_specs=[pl.BlockSpec(memory_space=pltpu.HBM)] * 3,
        scratch_shapes=[pltpu.VMEM(summed.shape, jnp.float32)] * 3
        + [pltpu.SemaphoreType.DMA((3,))],
        compiler_params=pltpu.CompilerParams(vmem_limit_bytes=16 * 1024 * 1024),
    )(summed, moment_m, moment_v)


def local(tokens_in, projector, gate_pre, up_pre, hidden_grad, moment_m, moment_v):
    ndp, nt = lax.axis_size("dp"), lax.axis_size("tensor")
    if fits(ndp, nt, tokens_in, projector, gate_pre):
        summed = exchange(ndp, nt, tokens_in, projector, gate_pre, up_pre, hidden_grad)
        return tuple(finish_call(summed, gate_pre.shape[0] * ndp, moment_m, moment_v))
    gate = gate_pre.astype(jnp.float32)
    hgrad = hidden_grad.astype(jnp.float32)
    sig = jax.nn.sigmoid(gate)
    upval = up_pre.astype(jnp.float32)
    grad_gate = (hgrad * upval * sig * (1.0 + gate * (1.0 - sig))).astype(jnp.bfloat16)
    grad_up = (hgrad * gate * sig).astype(jnp.bfloat16)
    grads = jnp.stack([grad_gate, grad_up])
    grads = lax.all_to_all(grads, "dp", split_axis=2, concat_axis=1, tiled=True)
    columns = lax.all_to_all(tokens_in, "tensor", split_axis=1, concat_axis=0, tiled=True)
    partial_xp = jnp.dot(columns, projector, preferred_element_type=jnp.float32)
    own_rows = lax.psum_scatter(partial_xp, "tensor", scatter_dimension=0, tiled=True).astype(
        jnp.bfloat16
    )
    xp = lax.all_gather(own_rows, ("dp", "tensor"), axis=0, tiled=True)
    contract = (((0,), (0,)), ((), ()))
    halves = [
        lax.dot_general(grads[k], xp, contract, preferred_element_type=jnp.float32) for k in (0, 1)
    ]
    summed = jnp.concatenate(halves, axis=1)
    return finish(summed, xp.shape[0], moment_m, moment_v)


def solution(mesh):
    return jax.shard_map(
        local,
        mesh=mesh,
        in_specs=(
            P(("dp", "tensor"), None),
            P("tensor", None),
            P("dp", "tensor"),
            P("dp", "tensor"),
            P("dp", "tensor"),
            P(("tensor", "dp"), None),
            P(("tensor", "dp"), None),
        ),
        out_specs=(P(("tensor", "dp"), None), P(("tensor", "dp"), None), P(("tensor", "dp"), None)),
        check_vma=False,
    )
```

```python
import functools

import jax
import jax.numpy as jnp
from jax import lax
from jax.experimental import pallas as pl
from jax.experimental.pallas import tpu as pltpu
from jax.sharding import PartitionSpec as P


MESH = pl.DeviceIdType.MESH
TAILS = 3
OUTER_EARLY = (
    ((1, 2, 0), (1, 0, 0), (0, 0, 1)),
    ((0, 0, 1), (1, 0, 0), (1, 2, 0)),
)
OUTER = (
    ((1, 3, 0), (1, 1, 0), (0, 1, 1), (1, 2, 1), (1, 0, 1), (1, 3, 1), (1, 1, 1)),
    ((0, 1, 1), (1, 1, 0), (1, 3, 0), (1, 0, 1), (1, 2, 1), (1, 1, 1), (1, 3, 1)),
)
INNER_EARLY = (
    ((0, 2, 0), (1, 0, 0), (1, 1, 0), 0),
    ((0, 3, 0), (1, 0, 0), (1, 1, 0), 0),
)
INNER = (
    ((0, 3, 0), (1, 0, 1), (0, 2, 1), (0, 3, 1), 1, 2, 3, 4, 5),
    ((0, 2, 0), (1, 0, 1), (0, 3, 1), (0, 2, 1), 1, 2, 3, 4, 5),
)
LATER = ((1, 1, 1),)
def pieces(rows):
    cuts = [-(-rows * i // (16 * TAILS)) * 16 for i in range(TAILS)] + [rows]
    return list(zip(cuts, cuts[1:]))


def exchange_kernel(
    ndp, nt, tok_ref, prj_ref, gate_ref, up_ref, hg_ref, out_ref,
    acts, prj_v, cols, part, rs_buf, xp_all, grads, recv,
    load_sem, tok_recv, rs_recv, xp_send,
    xz_recv, xt_recv, xc_recv, g_send, g_recv, cut_recv, near, late,
):
    d = lax.axis_index("dp")
    t = lax.axis_index("tensor")
    nz = ndp // 2
    z, c = d // 2, d % 2
    sub = tok_ref.shape[0]
    grp = sub * nt
    dcol = tok_ref.shape[1] // nt
    rows = recv.shape[2]
    rank = prj_ref.shape[1]
    half = ndp // 2
    half_tiles = half * rows // 128
    cut = pieces(rows)

    own_half = d // half
    inner = (z + 1) // 2 % 2
    up = z % 2
    adj = z + 1 - 2 * up
    far = (nz - 1) * (1 - z // 2)
    opp = 2 - z // 2
    first = own_half * (1 - inner) + (1 - own_half) * inner
    second = 1 - first

    def dest_of(which, j):
        return which * half + up * j + (1 - up) * (half - 1 - j)

    head = -(-rows // 128)
    spans = (
        (first, 0, 1), (first, 1, head), (first, head, half_tiles), (second, 0, half_tiles)
    )
    loads, places = [], []
    for i, (which, start, stop) in enumerate(spans):
        low = which * half_tiles + up * start + (1 - up) * (half_tiles - stop)
        at = pl.ds(pl.multiple_of(low * 128, 128), (stop - start) * 128)
        places.append(at)
        for k, src in enumerate((gate_ref, up_ref, hg_ref)):
            loads.append(
                pltpu.make_async_copy(src.at[:, at], acts.at[k, :, at], load_sem.at[min(i, 2)])
            )
    load_prj = pltpu.make_async_copy(prj_ref, prj_v, load_sem.at[0])
    own_tok = pltpu.make_async_copy(
        tok_ref.at[:, pl.ds(pl.multiple_of(t * dcol, 128), dcol)],
        cols.at[pl.ds(pl.multiple_of(t * sub, 16), sub), :],
        tok_recv.at[0],
    )
    for load in loads[:3]:
        load.start()

    def drain(ref, sem):
        pltpu.make_async_copy(ref, ref, sem).wait()

    barrier = pltpu.get_barrier_semaphore()

    def greet(dp, tensor):
        pl.semaphore_signal(barrier, inc=1, device_id=(dp, tensor), device_id_type=MESH)

    @pl.when(z < nz - 1)
    def _():
        for k in range(1, ndp):
            greet((d + k) % ndp, t)

    @pl.when(z == nz - 1)
    def _():
        greet(d + 1 - 2 * c, t)

    host = inner * adj + (1 - inner) * z
    for k in range(1, nt):
        greet(host * 2 + c, (t + k) % nt)

    for load in loads[3:]:
        load.start()
    own_tok.start()

    def tok_copy(dest, src):
        return pltpu.make_async_remote_copy(
            src_ref=tok_ref.at[:, pl.ds(pl.multiple_of(dest * dcol, 128), dcol)],
            dst_ref=cols.at[pl.ds(pl.multiple_of(src * sub, 16), sub), :],
            send_sem=xp_send.at[0],
            recv_sem=tok_recv.at[0],
            device_id=(d, dest),
            device_id_type=MESH,
        )

    def tile(i, carry):
        at = pl.ds(pl.multiple_of(i * 128, 128), 128)
        gate = acts[0, :, at].astype(jnp.float32)
        upval = acts[1, :, at].astype(jnp.float32)
        hgrad = acts[2, :, at].astype(jnp.float32)
        sig = jax.nn.sigmoid(gate)
        grad_gate = hgrad * upval * sig * (1.0 + gate * (1.0 - sig))
        grad_up = hgrad * gate * sig
        grads[0, at, :] = grad_gate.astype(jnp.bfloat16).T
        grads[1, at, :] = grad_up.astype(jnp.bfloat16).T
        return carry

    def tiles_of(which, start, stop):
        low = which * half_tiles + up * start + (1 - up) * (half_tiles - stop)
        lax.fori_loop(low, low + stop - start, tile, 0)

    def block_of(dest, side):
        return grads.at[side, pl.ds(pl.multiple_of(dest * rows, 16), rows), :]

    def grad_copy(dest, src, side):
        return pltpu.make_async_remote_copy(
            src_ref=block_of(dest, side),
            dst_ref=recv.at[src, side],
            send_sem=g_send.at[0],
            recv_sem=g_recv.at[src // 2],
            device_id=(dest, t),
            device_id_type=MESH,
        )

    def cut_copy(dest, src, p):
        start, stop = cut[p]
        at = pl.ds(pl.multiple_of(dest * rows + start, 16), stop - start)
        return pltpu.make_async_remote_copy(
            src_ref=grads.at[1, at, :],
            dst_ref=recv.at[src, 1, start:stop, :],
            send_sem=g_send.at[0],
            recv_sem=cut_recv.at[p],
            device_id=(dest, t),
            device_id_type=MESH,
        )

    def own_grad(side):
        return pltpu.make_async_copy(block_of(d, side), recv.at[d, side], g_recv.at[z])

    def send_near(dest, side):
        @pl.when(dest != d)
        def _():
            grad_copy(dest, d, side).start()

        @pl.when(dest == d)
        def _():
            own_grad(side).start()

    def send(which, j, side):
        grad_copy(dest_of(which, j), d, side).start()

    def send_all(kind, plans):
        for core, plan in enumerate(plans):

            @pl.when((inner == kind) & (c == core))
            def _():
                for item in plan:
                    if isinstance(item, int):
                        cut_copy(dest_of(first, item % 2), d, item // 2).start()
                    else:
                        send((first, second)[item[0]], *item[1:])

    def need(j):
        return -(-((j + 1) * rows) // 128)

    drain(acts.at[:, :, places[0]], load_sem.at[0])
    load_prj.start()
    tiles_of(first, 0, 1)
    known = jnp.where(z == nz - 1, ndp - 1, ndp - 3)
    pl.semaphore_wait(barrier, known + (1 - inner) * 2 * (nt - 1))

    def part_send(start, stop):
        low = dest_of(first, 0) * rows + up * start + (1 - up) * (rows - stop)
        at = pl.ds(pl.multiple_of(low, 16), stop - start)
        back = up * start + (1 - up) * (rows - stop)
        pltpu.make_async_remote_copy(
            src_ref=grads.at[0, at, :],
            dst_ref=recv.at[d, 0, pl.ds(pl.multiple_of(back, 16), stop - start), :],
            send_sem=g_send.at[0],
            recv_sem=g_recv.at[z],
            device_id=(dest_of(first, 0), t),
            device_id_type=MESH,
        ).start()

    def send_tokens():
        for k in range(1, nt):
            tok_copy((t + k) % nt, t).start()

    part_send(0, 128)

    @pl.when(inner == 0)
    def _():
        pl.semaphore_signal(near, inc=1, device_id=(adj * 2 + c, t), device_id_type=MESH)
        send_tokens()

    @pl.when(z == nz - 1)
    def _():
        for k in range(ndp - 2):
            pl.semaphore_signal(late, inc=1, device_id=(k, t), device_id_type=MESH)

    drain(acts.at[:, :, places[1]], load_sem.at[1])
    tiles_of(first, 1, head)
    part_send(128, rows)
    drain(acts.at[:, :, : (2 * half_tiles - head) * 128], load_sem.at[2])
    tiles_of(first, head, need(1))
    send(first, 1, 0)
    tiles_of(first, need(1), half_tiles)

    @pl.when(inner == 1)
    def _():
        pl.semaphore_wait(near, 1)
        send_tokens()

    tiles_of(second, 0, half_tiles)

    @pl.when(z < nz - 1)
    def _():
        pl.semaphore_wait(late, 2)

    send_all(0, OUTER_EARLY)
    send_all(1, INNER_EARLY)

    for j in (2, 3):
        for side in (0, 1):
            send_near(dest_of(own_half, j), side)

    load_prj.wait()
    drain(cols, tok_recv.at[0])
    drain(cols.at[: (nt - 1) * sub, :], xp_send.at[0])
    part[...] = jnp.dot(cols[...], prj_v[...], preferred_element_type=jnp.float32)

    def rs_copy(dest, src):
        return pltpu.make_async_remote_copy(
            src_ref=part.at[pl.ds(pl.multiple_of(dest * sub, 16), sub), :],
            dst_ref=rs_buf.at[src],
            send_sem=xp_send.at[0],
            recv_sem=rs_recv.at[0],
            device_id=(d, dest),
            device_id_type=MESH,
        )

    for k in range(1, nt):
        rs_copy((t + k) % nt, t).start()
    rs_buf[t] = part[pl.ds(pl.multiple_of(t * sub, 16), sub), :]
    drain(rs_buf.at[: nt - 1], rs_recv.at[0])
    drain(rs_buf.at[: nt - 1], xp_send.at[0])
    total = rs_buf[0]
    for k in range(1, nt):
        total = total + rs_buf[k]

    def piece(dd, tt):
        return xp_all.at[pl.ds(pl.multiple_of(dd * grp + tt * sub, 16), sub), :]

    xp_all[pl.ds(pl.multiple_of(d * grp + t * sub, 16), sub), :] = total.astype(jnp.bfloat16)

    def piece_copy(dd, tt, recv_sem, dest):
        return pltpu.make_async_remote_copy(
            src_ref=piece(dd, tt),
            dst_ref=piece(dd, tt),
            send_sem=xp_send.at[0],
            recv_sem=recv_sem,
            device_id=dest,
            device_id_type=MESH,
        )

    def along_z(zz, dest, slot):
        piece_copy(zz * 2 + c, t, xz_recv.at[slot], (dest * 2 + c, t)).start()

    along_z(z, opp, 1 + inner)
    along_z(z, adj, 0)

    send_all(0, OUTER)
    send_all(1, INNER)

    order = [z, adj, far, opp]

    for k, zz in enumerate(order):
        dd = zz * 2 + c
        if k:
            drain(piece(dd, t), xz_recv.at[k - 1])
        if k > 1:
            pl.when(inner == 1)(functools.partial(along_z, zz, adj, k - 1))
        for kt in range(1, nt):
            piece_copy(dd, t, xt_recv.at[k // 2], (d, (t + kt) % nt)).start()

    send_all(1, (LATER, LATER))

    partner = d + 1 - 2 * c

    def core_copy(zz, parity, slot):
        group = xp_all.at[pl.ds(pl.multiple_of((zz * 2 + parity) * grp, 128), grp), :]
        return pltpu.make_async_remote_copy(
            src_ref=group,
            dst_ref=group,
            send_sem=xp_send.at[0],
            recv_sem=xc_recv.at[slot],
            device_id=(partner, t),
            device_id_type=MESH,
        )

    for slot in (0, 1):
        drain(xp_all.at[: 2 * (nt - 1) * sub, :], xt_recv.at[slot])
        for zz in order[2 * slot : 2 * slot + 2]:
            core_copy(zz, c, slot).start()

    def add_term(k, zz, side, low, count):
        at = pl.ds(low, count)
        xp = xp_all[pl.ds(pl.multiple_of(zz * 2 * grp, 128), 2 * grp), :]
        lhs = jnp.concatenate([recv[zz * 2, side, at, :], recv[zz * 2 + 1, side, at, :]], axis=1)
        term = jnp.dot(lhs, xp, preferred_element_type=jnp.float32)
        cols_at = slice(side * rank, (side + 1) * rank)
        if k == 0:
            out_ref[at, cols_at] = term
        else:
            out_ref[at, cols_at] += term

    def take(k, zz):
        drain(recv.at[pl.ds(zz * 2, 2)], g_recv.at[zz])
        for side in (0, 1):
            add_term(k, zz, side, 0, rows)

    groups = xp_all.at[: 2 * grp, :]
    drain(groups, xc_recv.at[0])
    take(0, z)
    take(1, adj)
    drain(groups, xc_recv.at[1])
    moved = (nt - 1) * nz + nt * nz + 2
    pl.when(inner == 0)(lambda: drain(xp_all.at[: moved * sub, :], xp_send.at[0]))
    pl.when(inner == 1)(lambda: drain(xp_all.at[: (moved + 2) * sub, :], xp_send.at[0]))
    take(2, far)

    @pl.when(inner == 0)
    def _():
        take(3, opp)

    @pl.when(inner == 1)
    def _():
        drain(recv.at[pl.ds(opp * 2, 2), 0], g_recv.at[opp])
        add_term(3, opp, 0, 0, rows)
        for p, (start, stop) in enumerate(cut):
            drain(recv.at[pl.ds(opp * 2, 2), 1, start:stop, :], cut_recv.at[p])
            add_term(3, opp, 1, start, stop - start)

    drain(recv.at[: ndp - 1], g_send.at[0])


def exchange(ndp, nt, tokens_in, projector, gate_pre, up_pre, hidden_grad):
    sub, width = tokens_in.shape
    depth, rank = projector.shape
    grp, cols = gate_pre.shape
    rows = cols // ndp
    dma = pltpu.SemaphoreType.DMA
    bf, f32 = jnp.bfloat16, jnp.float32
    nz = ndp // 2
    operands = (tokens_in, projector, gate_pre, up_pre, hidden_grad)
    flops = 2 * grp * depth * rank + 4 * rows * grp * ndp * rank
    return pl.pallas_call(
        functools.partial(exchange_kernel, ndp, nt),
        out_shape=jax.ShapeDtypeStruct((rows, 2 * rank), f32),
        in_specs=[pl.BlockSpec(memory_space=pltpu.HBM)] * 5,
        out_specs=pl.BlockSpec(memory_space=pltpu.VMEM),
        scratch_shapes=[
            pltpu.VMEM((3, grp, cols), bf),
            pltpu.VMEM((depth, rank), bf),
            pltpu.VMEM((grp, depth), bf),
            pltpu.VMEM((grp, rank), f32),
            pltpu.VMEM((nt, sub, rank), f32),
            pltpu.VMEM((grp * ndp, rank), bf),
            pltpu.VMEM((2, cols, grp), bf),
            pltpu.VMEM((ndp, 2, rows, grp), bf),
            dma((3,)),
            dma((1,)),
            dma((1,)),
            dma((1,)),
            dma((3,)),
            dma((2,)),
            dma((2,)),
            dma((1,)),
            dma((nz,)),
            dma((TAILS,)),
            pltpu.SemaphoreType.REGULAR,
            pltpu.SemaphoreType.REGULAR,
        ],
        compiler_params=pltpu.CompilerParams(
            collective_id=0, has_side_effects=True, vmem_limit_bytes=32 * 1024 * 1024
        ),
        cost_estimate=pl.CostEstimate(
            flops=flops, bytes_accessed=8 * grp * cols, transcendentals=grp * cols
        ),
    )(*[pltpu.with_memory_space_constraint(x, pltpu.HBM) for x in operands])


def fits(ndp, nt, tokens_in, projector, gate_pre):
    sub, width = tokens_in.shape
    grp, cols = gate_pre.shape
    return (
        ndp == 8
        and nt >= 2
        and grp == 128
        and sub * nt == grp
        and sub % 16 == 0
        and cols % ndp == 0
        and (cols // ndp) % 16 == 0
        and cols // ndp >= 256
        and cols % 256 == 0
        and width % (128 * nt) == 0
        and projector.shape[0] == width // nt
        and projector.shape[1] % 128 == 0
        and cols <= 8192
        and projector.size <= 2**21
        and grp * ndp <= 4096
    )


def finish(summed, total_tokens, moment_m, moment_v):
    proj = summed * float(total_tokens) ** (-0.5)
    m_next = 0.9 * moment_m + 0.1 * proj
    v_next = 0.95 * moment_v + 0.05 * proj * proj
    direction = m_next / (jnp.sqrt(v_next) + 1e-08)
    return (m_next, v_next, direction)


def finish_kernel(total_tokens, steps, sum_ref, m_ref, v_ref, *refs):
    outs, bufs, sem = refs[:3], refs[3:6], refs[6]
    rows = sum_ref.shape[0] // steps
    for i in range(steps):
        at = slice(i * rows, (i + 1) * rows)
        values = finish(sum_ref[at, :], total_tokens, m_ref[at, :], v_ref[at, :])
        for k in range(3):
            bufs[k][at, :] = values[k]
            copy = pltpu.make_async_copy(
                bufs[k].at[at, :], outs[k].at[at, :], sem.at[k]
            )
            copy.start()
    for k in range(3):
        pltpu.make_async_copy(bufs[k], outs[k], sem.at[k]).wait()


def finish_call(summed, total_tokens, moment_m, moment_v):
    steps = 6
    shape = jax.ShapeDtypeStruct(summed.shape, jnp.float32)
    return pl.pallas_call(
        functools.partial(finish_kernel, total_tokens, steps),
        out_shape=(shape,) * 3,
        in_specs=[pl.BlockSpec(memory_space=pltpu.VMEM)] * 3,
        out_specs=[pl.BlockSpec(memory_space=pltpu.HBM)] * 3,
        scratch_shapes=[pltpu.VMEM(summed.shape, jnp.float32)] * 3
        + [pltpu.SemaphoreType.DMA((3,))],
        compiler_params=pltpu.CompilerParams(vmem_limit_bytes=16 * 1024 * 1024),
    )(summed, moment_m, moment_v)


def local(tokens_in, projector, gate_pre, up_pre, hidden_grad, moment_m, moment_v):
    ndp, nt = lax.axis_size("dp"), lax.axis_size("tensor")
    if fits(ndp, nt, tokens_in, projector, gate_pre):
        summed = exchange(ndp, nt, tokens_in, projector, gate_pre, up_pre, hidden_grad)
        return tuple(finish_call(summed, gate_pre.shape[0] * ndp, moment_m, moment_v))
    gate = gate_pre.astype(jnp.float32)
    hgrad = hidden_grad.astype(jnp.float32)
    sig = jax.nn.sigmoid(gate)
    upval = up_pre.astype(jnp.float32)
    grad_gate = (hgrad * upval * sig * (1.0 + gate * (1.0 - sig))).astype(jnp.bfloat16)
    grad_up = (hgrad * gate * sig).astype(jnp.bfloat16)
    grads = jnp.stack([grad_gate, grad_up])
    grads = lax.all_to_all(grads, "dp", split_axis=2, concat_axis=1, tiled=True)
    columns = lax.all_to_all(tokens_in, "tensor", split_axis=1, concat_axis=0, tiled=True)
    partial_xp = jnp.dot(columns, projector, preferred_element_type=jnp.float32)
    own_rows = lax.psum_scatter(partial_xp, "tensor", scatter_dimension=0, tiled=True).astype(
        jnp.bfloat16
    )
    xp = lax.all_gather(own_rows, ("dp", "tensor"), axis=0, tiled=True)
    contract = (((0,), (0,)), ((), ()))
    halves = [
        lax.dot_general(grads[k], xp, contract, preferred_element_type=jnp.float32) for k in (0, 1)
    ]
    summed = jnp.concatenate(halves, axis=1)
    return finish(summed, xp.shape[0], moment_m, moment_v)


def solution(mesh):
    return jax.shard_map(
        local,
        mesh=mesh,
        in_specs=(
            P(("dp", "tensor"), None),
            P("tensor", None),
            P("dp", "tensor"),
            P("dp", "tensor"),
            P("dp", "tensor"),
            P(("tensor", "dp"), None),
            P(("tensor", "dp"), None),
        ),
        out_specs=(P(("tensor", "dp"), None), P(("tensor", "dp"), None), P(("tensor", "dp"), None)),
        check_vma=False,
    )
```

```python
import functools

import jax
import jax.numpy as jnp
from jax import lax
from jax.experimental import pallas as pl
from jax.experimental.pallas import tpu as pltpu
from jax.sharding import PartitionSpec as P


MESH = pl.DeviceIdType.MESH
TAILS = 3
OUTER_EARLY = (
    ((1, 2, 0), (1, 0, 0), (0, 0, 1)),
    ((0, 0, 1), (1, 0, 0), (1, 2, 0)),
)
OUTER = (
    ((1, 3, 0), (1, 1, 0), (0, 1, 1), (1, 2, 1), (1, 0, 1), (1, 3, 1), (1, 1, 1)),
    ((0, 1, 1), (1, 1, 0), (1, 3, 0), (1, 0, 1), (1, 2, 1), (1, 1, 1), (1, 3, 1)),
)
INNER_EARLY = (
    ((0, 2, 0), (1, 0, 0), (1, 1, 0), 0),
    ((0, 3, 0), (1, 0, 0), (1, 1, 0), 0),
)
INNER = (
    ((0, 3, 0), (1, 0, 1), (0, 2, 1), (0, 3, 1), 1, 2, 3, 4, 5),
    ((0, 2, 0), (1, 0, 1), (0, 3, 1), (0, 2, 1), 1, 2, 3, 4, 5),
)
LATER = ((1, 1, 1),)
def pieces(rows):
    cuts = [-(-rows * i // (16 * TAILS)) * 16 for i in range(TAILS)] + [rows]
    return list(zip(cuts, cuts[1:]))


def exchange_kernel(
    ndp, nt, tok_ref, prj_ref, gate_ref, up_ref, hg_ref, m_ref, v_ref, out_ref, m_out, v_out,
    acts, prj_v, cols, part, rs_buf, xp_all, grads, recv,
    load_sem, tok_recv, rs_recv, xp_send,
    xz_recv, xt_recv, xc_recv, g_send, g_recv, cut_recv, near, late,
):
    d = lax.axis_index("dp")
    t = lax.axis_index("tensor")
    nz = ndp // 2
    z, c = d // 2, d % 2
    sub = tok_ref.shape[0]
    grp = sub * nt
    dcol = tok_ref.shape[1] // nt
    rows = recv.shape[2]
    rank = prj_ref.shape[1]
    half = ndp // 2
    half_tiles = half * rows // 128
    cut = pieces(rows)

    own_half = d // half
    inner = (z + 1) // 2 % 2
    up = z % 2
    adj = z + 1 - 2 * up
    far = (nz - 1) * (1 - z // 2)
    opp = 2 - z // 2
    first = own_half * (1 - inner) + (1 - own_half) * inner
    second = 1 - first

    def dest_of(which, j):
        return which * half + up * j + (1 - up) * (half - 1 - j)

    head = -(-rows // 128)
    spans = (
        (first, 0, 1), (first, 1, head), (first, head, half_tiles), (second, 0, half_tiles)
    )
    loads, places = [], []
    for i, (which, start, stop) in enumerate(spans):
        low = which * half_tiles + up * start + (1 - up) * (half_tiles - stop)
        at = pl.ds(pl.multiple_of(low * 128, 128), (stop - start) * 128)
        places.append(at)
        for k, src in enumerate((gate_ref, up_ref, hg_ref)):
            loads.append(
                pltpu.make_async_copy(src.at[:, at], acts.at[k, :, at], load_sem.at[min(i, 2)])
            )
    load_prj = pltpu.make_async_copy(prj_ref, prj_v, load_sem.at[0])
    own_tok = pltpu.make_async_copy(
        tok_ref.at[:, pl.ds(pl.multiple_of(t * dcol, 128), dcol)],
        cols.at[pl.ds(pl.multiple_of(t * sub, 16), sub), :],
        tok_recv.at[0],
    )
    for load in loads[:3]:
        load.start()

    def drain(ref, sem):
        pltpu.make_async_copy(ref, ref, sem).wait()

    barrier = pltpu.get_barrier_semaphore()

    def greet(dp, tensor):
        pl.semaphore_signal(barrier, inc=1, device_id=(dp, tensor), device_id_type=MESH)

    @pl.when(z < nz - 1)
    def _():
        for k in range(1, ndp):
            greet((d + k) % ndp, t)

    @pl.when(z == nz - 1)
    def _():
        greet(d + 1 - 2 * c, t)

    host = inner * adj + (1 - inner) * z
    for k in range(1, nt):
        greet(host * 2 + c, (t + k) % nt)

    for load in loads[3:]:
        load.start()
    own_tok.start()

    def tok_copy(dest, src):
        return pltpu.make_async_remote_copy(
            src_ref=tok_ref.at[:, pl.ds(pl.multiple_of(dest * dcol, 128), dcol)],
            dst_ref=cols.at[pl.ds(pl.multiple_of(src * sub, 16), sub), :],
            send_sem=xp_send.at[0],
            recv_sem=tok_recv.at[0],
            device_id=(d, dest),
            device_id_type=MESH,
        )

    def tile(i, carry):
        at = pl.ds(pl.multiple_of(i * 128, 128), 128)
        gate = acts[0, :, at].astype(jnp.float32)
        upval = acts[1, :, at].astype(jnp.float32)
        hgrad = acts[2, :, at].astype(jnp.float32)
        sig = jax.nn.sigmoid(gate)
        grad_gate = hgrad * upval * sig * (1.0 + gate * (1.0 - sig))
        grad_up = hgrad * gate * sig
        grads[0, at, :] = grad_gate.astype(jnp.bfloat16).T
        grads[1, at, :] = grad_up.astype(jnp.bfloat16).T
        return carry

    def tiles_of(which, start, stop):
        low = which * half_tiles + up * start + (1 - up) * (half_tiles - stop)
        lax.fori_loop(low, low + stop - start, tile, 0)

    def block_of(dest, side):
        return grads.at[side, pl.ds(pl.multiple_of(dest * rows, 16), rows), :]

    def grad_copy(dest, src, side):
        return pltpu.make_async_remote_copy(
            src_ref=block_of(dest, side),
            dst_ref=recv.at[src, side],
            send_sem=g_send.at[0],
            recv_sem=g_recv.at[src // 2],
            device_id=(dest, t),
            device_id_type=MESH,
        )

    def cut_copy(dest, src, p):
        start, stop = cut[p]
        at = pl.ds(pl.multiple_of(dest * rows + start, 16), stop - start)
        return pltpu.make_async_remote_copy(
            src_ref=grads.at[1, at, :],
            dst_ref=recv.at[src, 1, start:stop, :],
            send_sem=g_send.at[0],
            recv_sem=cut_recv.at[p],
            device_id=(dest, t),
            device_id_type=MESH,
        )

    def own_grad(side):
        return pltpu.make_async_copy(block_of(d, side), recv.at[d, side], g_recv.at[z])

    def send_near(dest, side):
        @pl.when(dest != d)
        def _():
            grad_copy(dest, d, side).start()

        @pl.when(dest == d)
        def _():
            own_grad(side).start()

    def send(which, j, side):
        grad_copy(dest_of(which, j), d, side).start()

    def send_all(kind, plans):
        for core, plan in enumerate(plans):

            @pl.when((inner == kind) & (c == core))
            def _():
                for item in plan:
                    if isinstance(item, int):
                        cut_copy(dest_of(first, item % 2), d, item // 2).start()
                    else:
                        send((first, second)[item[0]], *item[1:])

    def need(j):
        return -(-((j + 1) * rows) // 128)

    drain(acts.at[:, :, places[0]], load_sem.at[0])
    load_prj.start()
    tiles_of(first, 0, 1)
    known = jnp.where(z == nz - 1, ndp - 1, ndp - 3)
    pl.semaphore_wait(barrier, known + (1 - inner) * 2 * (nt - 1))

    def part_send(start, stop):
        low = dest_of(first, 0) * rows + up * start + (1 - up) * (rows - stop)
        at = pl.ds(pl.multiple_of(low, 16), stop - start)
        back = up * start + (1 - up) * (rows - stop)
        pltpu.make_async_remote_copy(
            src_ref=grads.at[0, at, :],
            dst_ref=recv.at[d, 0, pl.ds(pl.multiple_of(back, 16), stop - start), :],
            send_sem=g_send.at[0],
            recv_sem=g_recv.at[z],
            device_id=(dest_of(first, 0), t),
            device_id_type=MESH,
        ).start()

    def send_tokens():
        for k in range(1, nt):
            tok_copy((t + k) % nt, t).start()

    part_send(0, 128)

    @pl.when(inner == 0)
    def _():
        pl.semaphore_signal(near, inc=1, device_id=(adj * 2 + c, t), device_id_type=MESH)
        send_tokens()

    @pl.when(z == nz - 1)
    def _():
        for k in range(ndp - 2):
            pl.semaphore_signal(late, inc=1, device_id=(k, t), device_id_type=MESH)

    drain(acts.at[:, :, places[1]], load_sem.at[1])
    tiles_of(first, 1, head)
    part_send(128, rows)
    drain(acts.at[:, :, : (2 * half_tiles - head) * 128], load_sem.at[2])
    tiles_of(first, head, need(1))
    send(first, 1, 0)
    tiles_of(first, need(1), half_tiles)

    @pl.when(inner == 1)
    def _():
        pl.semaphore_wait(near, 1)
        send_tokens()

    tiles_of(second, 0, half_tiles)

    @pl.when(z < nz - 1)
    def _():
        pl.semaphore_wait(late, 2)

    send_all(0, OUTER_EARLY)
    send_all(1, INNER_EARLY)

    for j in (2, 3):
        for side in (0, 1):
            send_near(dest_of(own_half, j), side)

    load_prj.wait()
    moments = [
        pltpu.make_async_copy(m_ref, m_out, load_sem.at[1]),
        pltpu.make_async_copy(v_ref, v_out, load_sem.at[2]),
    ]
    for load in moments:
        load.start()
    drain(cols, tok_recv.at[0])
    drain(cols.at[: (nt - 1) * sub, :], xp_send.at[0])
    part[...] = jnp.dot(cols[...], prj_v[...], preferred_element_type=jnp.float32)

    def rs_copy(dest, src):
        return pltpu.make_async_remote_copy(
            src_ref=part.at[pl.ds(pl.multiple_of(dest * sub, 16), sub), :],
            dst_ref=rs_buf.at[src],
            send_sem=xp_send.at[0],
            recv_sem=rs_recv.at[0],
            device_id=(d, dest),
            device_id_type=MESH,
        )

    for k in range(1, nt):
        rs_copy((t + k) % nt, t).start()
    rs_buf[t] = part[pl.ds(pl.multiple_of(t * sub, 16), sub), :]
    drain(rs_buf.at[: nt - 1], rs_recv.at[0])
    drain(rs_buf.at[: nt - 1], xp_send.at[0])
    total = rs_buf[0]
    for k in range(1, nt):
        total = total + rs_buf[k]

    def piece(dd, tt):
        return xp_all.at[pl.ds(pl.multiple_of(dd * grp + tt * sub, 16), sub), :]

    xp_all[pl.ds(pl.multiple_of(d * grp + t * sub, 16), sub), :] = total.astype(jnp.bfloat16)

    def piece_copy(dd, tt, recv_sem, dest):
        return pltpu.make_async_remote_copy(
            src_ref=piece(dd, tt),
            dst_ref=piece(dd, tt),
            send_sem=xp_send.at[0],
            recv_sem=recv_sem,
            device_id=dest,
            device_id_type=MESH,
        )

    def along_z(zz, dest, slot):
        piece_copy(zz * 2 + c, t, xz_recv.at[slot], (dest * 2 + c, t)).start()

    along_z(z, opp, 1 + inner)
    along_z(z, adj, 0)

    send_all(0, OUTER)
    send_all(1, INNER)

    order = [z, adj, far, opp]

    for k, zz in enumerate(order):
        dd = zz * 2 + c
        if k:
            drain(piece(dd, t), xz_recv.at[k - 1])
        if k > 1:
            pl.when(inner == 1)(functools.partial(along_z, zz, adj, k - 1))
        for kt in range(1, nt):
            piece_copy(dd, t, xt_recv.at[k // 2], (d, (t + kt) % nt)).start()

    send_all(1, (LATER, LATER))

    partner = d + 1 - 2 * c

    def core_copy(zz, parity, slot):
        group = xp_all.at[pl.ds(pl.multiple_of((zz * 2 + parity) * grp, 128), grp), :]
        return pltpu.make_async_remote_copy(
            src_ref=group,
            dst_ref=group,
            send_sem=xp_send.at[0],
            recv_sem=xc_recv.at[slot],
            device_id=(partner, t),
            device_id_type=MESH,
        )

    for slot in (0, 1):
        drain(xp_all.at[: 2 * (nt - 1) * sub, :], xt_recv.at[slot])
        for zz in order[2 * slot : 2 * slot + 2]:
            core_copy(zz, c, slot).start()

    def add_term(k, zz, side, low, count):
        at = pl.ds(low, count)
        xp = xp_all[pl.ds(pl.multiple_of(zz * 2 * grp, 128), 2 * grp), :]
        lhs = jnp.concatenate([recv[zz * 2, side, at, :], recv[zz * 2 + 1, side, at, :]], axis=1)
        term = jnp.dot(lhs, xp, preferred_element_type=jnp.float32)
        cols_at = slice(side * rank, (side + 1) * rank)
        if k == 0:
            out_ref[at, cols_at] = term
        else:
            out_ref[at, cols_at] += term

    def take(k, zz):
        drain(recv.at[pl.ds(zz * 2, 2)], g_recv.at[zz])
        for side in (0, 1):
            add_term(k, zz, side, 0, rows)

    groups = xp_all.at[: 2 * grp, :]
    drain(groups, xc_recv.at[0])
    take(0, z)
    take(1, adj)
    drain(groups, xc_recv.at[1])
    for load in moments:
        load.wait()
    moved = (nt - 1) * nz + nt * nz + 2
    pl.when(inner == 0)(lambda: drain(xp_all.at[: moved * sub, :], xp_send.at[0]))
    pl.when(inner == 1)(lambda: drain(xp_all.at[: (moved + 2) * sub, :], xp_send.at[0]))
    take(2, far)

    @pl.when(inner == 0)
    def _():
        take(3, opp)

    @pl.when(inner == 1)
    def _():
        drain(recv.at[pl.ds(opp * 2, 2), 0], g_recv.at[opp])
        add_term(3, opp, 0, 0, rows)
        for p, (start, stop) in enumerate(cut):
            drain(recv.at[pl.ds(opp * 2, 2), 1, start:stop, :], cut_recv.at[p])
            add_term(3, opp, 1, start, stop - start)

    drain(recv.at[: ndp - 1], g_send.at[0])


def exchange(ndp, nt, tokens_in, projector, gate_pre, up_pre, hidden_grad, moment_m, moment_v):
    sub, width = tokens_in.shape
    depth, rank = projector.shape
    grp, cols = gate_pre.shape
    rows = cols // ndp
    dma = pltpu.SemaphoreType.DMA
    bf, f32 = jnp.bfloat16, jnp.float32
    nz = ndp // 2
    operands = (tokens_in, projector, gate_pre, up_pre, hidden_grad, moment_m, moment_v)
    flops = 2 * grp * depth * rank + 4 * rows * grp * ndp * rank
    return pl.pallas_call(
        functools.partial(exchange_kernel, ndp, nt),
        out_shape=(jax.ShapeDtypeStruct((rows, 2 * rank), f32),) * 3,
        in_specs=[pl.BlockSpec(memory_space=pltpu.HBM)] * 7,
        out_specs=(pl.BlockSpec(memory_space=pltpu.VMEM),) * 3,
        scratch_shapes=[
            pltpu.VMEM((3, grp, cols), bf),
            pltpu.VMEM((depth, rank), bf),
            pltpu.VMEM((grp, depth), bf),
            pltpu.VMEM((grp, rank), f32),
            pltpu.VMEM((nt, sub, rank), f32),
            pltpu.VMEM((grp * ndp, rank), bf),
            pltpu.VMEM((2, cols, grp), bf),
            pltpu.VMEM((ndp, 2, rows, grp), bf),
            dma((3,)),
            dma((1,)),
            dma((1,)),
            dma((1,)),
            dma((3,)),
            dma((2,)),
            dma((2,)),
            dma((1,)),
            dma((nz,)),
            dma((TAILS,)),
            pltpu.SemaphoreType.REGULAR,
            pltpu.SemaphoreType.REGULAR,
        ],
        compiler_params=pltpu.CompilerParams(
            collective_id=0, has_side_effects=True, vmem_limit_bytes=32 * 1024 * 1024
        ),
        cost_estimate=pl.CostEstimate(
            flops=flops, bytes_accessed=8 * grp * cols, transcendentals=grp * cols
        ),
    )(*[pltpu.with_memory_space_constraint(x, pltpu.HBM) for x in operands])


def fits(ndp, nt, tokens_in, projector, gate_pre):
    sub, width = tokens_in.shape
    grp, cols = gate_pre.shape
    return (
        ndp == 8
        and nt >= 2
        and grp == 128
        and sub * nt == grp
        and sub % 16 == 0
        and cols % ndp == 0
        and (cols // ndp) % 16 == 0
        and cols // ndp >= 256
        and cols % 256 == 0
        and width % (128 * nt) == 0
        and projector.shape[0] == width // nt
        and projector.shape[1] % 128 == 0
        and cols <= 8192
        and projector.size <= 2**21
        and grp * ndp <= 4096
    )


def finish(summed, total_tokens, moment_m, moment_v):
    proj = summed * float(total_tokens) ** (-0.5)
    m_next = 0.9 * moment_m + 0.1 * proj
    v_next = 0.95 * moment_v + 0.05 * proj * proj
    direction = m_next / (jnp.sqrt(v_next) + 1e-08)
    return (m_next, v_next, direction)


def finish_kernel(total_tokens, steps, sum_ref, m_ref, v_ref, *refs):
    outs, bufs, sem = refs[:3], refs[3:6], refs[6]
    rows = sum_ref.shape[0] // steps
    for i in range(steps):
        at = slice(i * rows, (i + 1) * rows)
        values = finish(sum_ref[at, :], total_tokens, m_ref[at, :], v_ref[at, :])
        for k in range(3):
            bufs[k][at, :] = values[k]
            copy = pltpu.make_async_copy(
                bufs[k].at[at, :], outs[k].at[at, :], sem.at[k]
            )
            copy.start()
    for k in range(3):
        pltpu.make_async_copy(bufs[k], outs[k], sem.at[k]).wait()


def finish_call(summed, moment_m, moment_v, total_tokens):
    steps = 6
    shape = jax.ShapeDtypeStruct(summed.shape, jnp.float32)
    return pl.pallas_call(
        functools.partial(finish_kernel, total_tokens, steps),
        out_shape=(shape,) * 3,
        in_specs=[pl.BlockSpec(memory_space=pltpu.VMEM)] * 3,
        out_specs=[pl.BlockSpec(memory_space=pltpu.HBM)] * 3,
        scratch_shapes=[pltpu.VMEM(summed.shape, jnp.float32)] * 3
        + [pltpu.SemaphoreType.DMA((3,))],
        compiler_params=pltpu.CompilerParams(vmem_limit_bytes=16 * 1024 * 1024),
    )(summed, moment_m, moment_v)


def local(tokens_in, projector, gate_pre, up_pre, hidden_grad, moment_m, moment_v):
    ndp, nt = lax.axis_size("dp"), lax.axis_size("tensor")
    if fits(ndp, nt, tokens_in, projector, gate_pre):
        operands = tokens_in, projector, gate_pre, up_pre, hidden_grad, moment_m, moment_v
        return tuple(finish_call(*exchange(ndp, nt, *operands), gate_pre.shape[0] * ndp))
    gate = gate_pre.astype(jnp.float32)
    hgrad = hidden_grad.astype(jnp.float32)
    sig = jax.nn.sigmoid(gate)
    upval = up_pre.astype(jnp.float32)
    grad_gate = (hgrad * upval * sig * (1.0 + gate * (1.0 - sig))).astype(jnp.bfloat16)
    grad_up = (hgrad * gate * sig).astype(jnp.bfloat16)
    grads = jnp.stack([grad_gate, grad_up])
    grads = lax.all_to_all(grads, "dp", split_axis=2, concat_axis=1, tiled=True)
    columns = lax.all_to_all(tokens_in, "tensor", split_axis=1, concat_axis=0, tiled=True)
    partial_xp = jnp.dot(columns, projector, preferred_element_type=jnp.float32)
    own_rows = lax.psum_scatter(partial_xp, "tensor", scatter_dimension=0, tiled=True).astype(
        jnp.bfloat16
    )
    xp = lax.all_gather(own_rows, ("dp", "tensor"), axis=0, tiled=True)
    contract = (((0,), (0,)), ((), ()))
    halves = [
        lax.dot_general(grads[k], xp, contract, preferred_element_type=jnp.float32) for k in (0, 1)
    ]
    summed = jnp.concatenate(halves, axis=1)
    return finish(summed, xp.shape[0], moment_m, moment_v)


def solution(mesh):
    return jax.shard_map(
        local,
        mesh=mesh,
        in_specs=(
            P(("dp", "tensor"), None),
            P("tensor", None),
            P("dp", "tensor"),
            P("dp", "tensor"),
            P("dp", "tensor"),
            P(("tensor", "dp"), None),
            P(("tensor", "dp"), None),
        ),
        out_specs=(P(("tensor", "dp"), None), P(("tensor", "dp"), None), P(("tensor", "dp"), None)),
        check_vma=False,
    )
```

```python
import functools

import jax
import jax.numpy as jnp
from jax import lax
from jax.experimental import pallas as pl
from jax.experimental.pallas import tpu as pltpu
from jax.sharding import PartitionSpec as P


MESH = pl.DeviceIdType.MESH
TAILS = 3
OUTER_EARLY = (
    ((1, 2, 0), (1, 0, 0), (0, 0, 1)),
    ((0, 0, 1), (1, 0, 0), (1, 2, 0)),
)
OUTER = (
    ((1, 3, 0), (1, 1, 0), (0, 1, 1), (1, 2, 1), (1, 0, 1), (1, 3, 1), (1, 1, 1)),
    ((0, 1, 1), (1, 1, 0), (1, 3, 0), (1, 0, 1), (1, 2, 1), (1, 1, 1), (1, 3, 1)),
)
INNER_EARLY = (
    ((0, 2, 0), (1, 0, 0), (1, 1, 0), 0),
    ((0, 3, 0), (1, 0, 0), (1, 1, 0), 0),
)
INNER = (
    ((0, 3, 0), (1, 0, 1), (0, 2, 1), (0, 3, 1), 1, 2, 3, 4, 5),
    ((0, 2, 0), (1, 0, 1), (0, 3, 1), (0, 2, 1), 1, 2, 3, 4, 5),
)
LATER = ((1, 1, 1),)
def pieces(rows):
    cuts = [-(-rows * i // (16 * TAILS)) * 16 for i in range(TAILS)] + [rows]
    return list(zip(cuts, cuts[1:]))


def exchange_kernel(
    ndp, nt, tok_ref, prj_ref, gate_ref, up_ref, hg_ref, m_ref, v_ref, out_ref, m_out, v_out,
    acts, prj_v, cols, part, rs_buf, xp_all, grads, recv,
    load_sem, tok_recv, rs_recv, xp_send,
    xz_recv, xt_recv, xc_recv, g_send, g_recv, cut_recv, near, late,
):
    d = lax.axis_index("dp")
    t = lax.axis_index("tensor")
    nz = ndp // 2
    z, c = d // 2, d % 2
    sub = tok_ref.shape[0]
    grp = sub * nt
    dcol = tok_ref.shape[1] // nt
    rows = recv.shape[2]
    rank = prj_ref.shape[1]
    half = ndp // 2
    half_tiles = half * rows // 128
    cut = pieces(rows)

    own_half = d // half
    inner = (z + 1) // 2 % 2
    up = z % 2
    adj = z + 1 - 2 * up
    far = (nz - 1) * (1 - z // 2)
    opp = 2 - z // 2
    first = own_half * (1 - inner) + (1 - own_half) * inner
    second = 1 - first

    def dest_of(which, j):
        return which * half + up * j + (1 - up) * (half - 1 - j)

    head = -(-rows // 128)
    spans = (
        (first, 0, 1), (first, 1, head), (first, head, half_tiles), (second, 0, half_tiles)
    )
    loads, places = [], []
    for i, (which, start, stop) in enumerate(spans):
        low = which * half_tiles + up * start + (1 - up) * (half_tiles - stop)
        at = pl.ds(pl.multiple_of(low * 128, 128), (stop - start) * 128)
        places.append(at)
        for k, src in enumerate((gate_ref, up_ref, hg_ref)):
            loads.append(
                pltpu.make_async_copy(src.at[:, at], acts.at[k, :, at], load_sem.at[min(i, 2)])
            )
    load_prj = pltpu.make_async_copy(prj_ref, prj_v, load_sem.at[0])
    own_tok = pltpu.make_async_copy(
        tok_ref.at[:, pl.ds(pl.multiple_of(t * dcol, 128), dcol)],
        cols.at[pl.ds(pl.multiple_of(t * sub, 16), sub), :],
        tok_recv.at[0],
    )
    for load in loads[:3]:
        load.start()

    def drain(ref, sem):
        pltpu.make_async_copy(ref, ref, sem).wait()

    barrier = pltpu.get_barrier_semaphore()

    def greet(dp, tensor):
        pl.semaphore_signal(barrier, inc=1, device_id=(dp, tensor), device_id_type=MESH)

    @pl.when(z < nz - 1)
    def _():
        for k in range(1, ndp):
            greet((d + k) % ndp, t)

    @pl.when(z == nz - 1)
    def _():
        greet(d + 1 - 2 * c, t)

    host = inner * adj + (1 - inner) * z
    for k in range(1, nt):
        greet(host * 2 + c, (t + k) % nt)

    for load in loads[3:]:
        load.start()
    own_tok.start()

    def tok_copy(dest, src):
        return pltpu.make_async_remote_copy(
            src_ref=tok_ref.at[:, pl.ds(pl.multiple_of(dest * dcol, 128), dcol)],
            dst_ref=cols.at[pl.ds(pl.multiple_of(src * sub, 16), sub), :],
            send_sem=xp_send.at[0],
            recv_sem=tok_recv.at[0],
            device_id=(d, dest),
            device_id_type=MESH,
        )

    def tile(i, carry):
        at = pl.ds(pl.multiple_of(i * 128, 128), 128)
        gate = acts[0, :, at].astype(jnp.float32)
        upval = acts[1, :, at].astype(jnp.float32)
        hgrad = acts[2, :, at].astype(jnp.float32)
        sig = jax.nn.sigmoid(gate)
        grad_gate = hgrad * upval * sig * (1.0 + gate * (1.0 - sig))
        grad_up = hgrad * gate * sig
        grads[0, at, :] = grad_gate.astype(jnp.bfloat16).T
        grads[1, at, :] = grad_up.astype(jnp.bfloat16).T
        return carry

    def tiles_of(which, start, stop):
        low = which * half_tiles + up * start + (1 - up) * (half_tiles - stop)
        lax.fori_loop(low, low + stop - start, tile, 0)

    def block_of(dest, side):
        return grads.at[side, pl.ds(pl.multiple_of(dest * rows, 16), rows), :]

    def grad_copy(dest, src, side):
        return pltpu.make_async_remote_copy(
            src_ref=block_of(dest, side),
            dst_ref=recv.at[src, side],
            send_sem=g_send.at[0],
            recv_sem=g_recv.at[src // 2],
            device_id=(dest, t),
            device_id_type=MESH,
        )

    def cut_copy(dest, src, p):
        start, stop = cut[p]
        at = pl.ds(pl.multiple_of(dest * rows + start, 16), stop - start)
        return pltpu.make_async_remote_copy(
            src_ref=grads.at[1, at, :],
            dst_ref=recv.at[src, 1, start:stop, :],
            send_sem=g_send.at[0],
            recv_sem=cut_recv.at[p],
            device_id=(dest, t),
            device_id_type=MESH,
        )

    def own_grad(side):
        return pltpu.make_async_copy(block_of(d, side), recv.at[d, side], g_recv.at[z])

    def send_near(dest, side):
        @pl.when(dest != d)
        def _():
            grad_copy(dest, d, side).start()

        @pl.when(dest == d)
        def _():
            own_grad(side).start()

    def send(which, j, side):
        grad_copy(dest_of(which, j), d, side).start()

    def send_all(kind, plans):
        for core, plan in enumerate(plans):

            @pl.when((inner == kind) & (c == core))
            def _():
                for item in plan:
                    if isinstance(item, int):
                        cut_copy(dest_of(first, item % 2), d, item // 2).start()
                    else:
                        send((first, second)[item[0]], *item[1:])

    def need(j):
        return -(-((j + 1) * rows) // 128)

    drain(acts.at[:, :, places[0]], load_sem.at[0])
    load_prj.start()
    tiles_of(first, 0, 1)
    known = jnp.where(z == nz - 1, ndp - 1, ndp - 3)
    pl.semaphore_wait(barrier, known + (1 - inner) * 2 * (nt - 1))

    def part_send(start, stop):
        low = dest_of(first, 0) * rows + up * start + (1 - up) * (rows - stop)
        at = pl.ds(pl.multiple_of(low, 16), stop - start)
        back = up * start + (1 - up) * (rows - stop)
        pltpu.make_async_remote_copy(
            src_ref=grads.at[0, at, :],
            dst_ref=recv.at[d, 0, pl.ds(pl.multiple_of(back, 16), stop - start), :],
            send_sem=g_send.at[0],
            recv_sem=g_recv.at[z],
            device_id=(dest_of(first, 0), t),
            device_id_type=MESH,
        ).start()

    def send_tokens():
        for k in range(1, nt):
            tok_copy((t + k) % nt, t).start()

    part_send(0, 128)

    @pl.when(inner == 0)
    def _():
        pl.semaphore_signal(near, inc=1, device_id=(adj * 2 + c, t), device_id_type=MESH)
        send_tokens()

    @pl.when(z == nz - 1)
    def _():
        for k in range(ndp - 2):
            pl.semaphore_signal(late, inc=1, device_id=(k, t), device_id_type=MESH)

    drain(acts.at[:, :, places[1]], load_sem.at[1])
    tiles_of(first, 1, head)
    part_send(128, rows)
    drain(acts.at[:, :, : (2 * half_tiles - head) * 128], load_sem.at[2])
    tiles_of(first, head, need(1))
    send(first, 1, 0)
    tiles_of(first, need(1), half_tiles)

    @pl.when(inner == 1)
    def _():
        pl.semaphore_wait(near, 1)
        send_tokens()

    tiles_of(second, 0, half_tiles)

    @pl.when(z < nz - 1)
    def _():
        pl.semaphore_wait(late, 2)

    send_all(0, OUTER_EARLY)
    send_all(1, INNER_EARLY)

    for j in (2, 3):
        for side in (0, 1):
            send_near(dest_of(own_half, j), side)

    load_prj.wait()
    moments = [
        pltpu.make_async_copy(m_ref, m_out, load_sem.at[1]),
        pltpu.make_async_copy(v_ref, v_out, load_sem.at[2]),
    ]
    for load in moments:
        load.start()
    drain(cols, tok_recv.at[0])
    drain(cols.at[: (nt - 1) * sub, :], xp_send.at[0])
    part[...] = jnp.dot(cols[...], prj_v[...], preferred_element_type=jnp.float32)

    def rs_copy(dest, src):
        return pltpu.make_async_remote_copy(
            src_ref=part.at[pl.ds(pl.multiple_of(dest * sub, 16), sub), :],
            dst_ref=rs_buf.at[src],
            send_sem=xp_send.at[0],
            recv_sem=rs_recv.at[0],
            device_id=(d, dest),
            device_id_type=MESH,
        )

    for k in range(1, nt):
        rs_copy((t + k) % nt, t).start()
    rs_buf[t] = part[pl.ds(pl.multiple_of(t * sub, 16), sub), :]
    drain(rs_buf.at[: nt - 1], rs_recv.at[0])
    drain(rs_buf.at[: nt - 1], xp_send.at[0])
    total = rs_buf[0]
    for k in range(1, nt):
        total = total + rs_buf[k]

    def piece(dd, tt):
        return xp_all.at[pl.ds(pl.multiple_of(dd * grp + tt * sub, 16), sub), :]

    xp_all[pl.ds(pl.multiple_of(d * grp + t * sub, 16), sub), :] = total.astype(jnp.bfloat16)

    def piece_copy(dd, tt, recv_sem, dest):
        return pltpu.make_async_remote_copy(
            src_ref=piece(dd, tt),
            dst_ref=piece(dd, tt),
            send_sem=xp_send.at[0],
            recv_sem=recv_sem,
            device_id=dest,
            device_id_type=MESH,
        )

    def along_z(zz, dest, slot):
        piece_copy(zz * 2 + c, t, xz_recv.at[slot], (dest * 2 + c, t)).start()

    along_z(z, opp, 1 + inner)
    along_z(z, adj, 0)

    send_all(0, OUTER)
    send_all(1, INNER)

    order = [z, adj, far, opp]

    for k, zz in enumerate(order):
        dd = zz * 2 + c
        if k:
            drain(piece(dd, t), xz_recv.at[k - 1])
        if k > 1:
            pl.when(inner == 1)(functools.partial(along_z, zz, adj, k - 1))
        for kt in range(1, nt):
            piece_copy(dd, t, xt_recv.at[k // 2], (d, (t + kt) % nt)).start()

    send_all(1, (LATER, LATER))

    partner = d + 1 - 2 * c

    def core_copy(zz, parity, slot):
        group = xp_all.at[pl.ds(pl.multiple_of((zz * 2 + parity) * grp, 128), grp), :]
        return pltpu.make_async_remote_copy(
            src_ref=group,
            dst_ref=group,
            send_sem=xp_send.at[0],
            recv_sem=xc_recv.at[slot],
            device_id=(partner, t),
            device_id_type=MESH,
        )

    for slot in (0, 1):
        drain(xp_all.at[: 2 * (nt - 1) * sub, :], xt_recv.at[slot])
        for zz in order[2 * slot : 2 * slot + 2]:
            core_copy(zz, c, slot).start()

    def add_term(k, zz, side, low, count):
        at = pl.ds(low, count)
        xp = xp_all[pl.ds(pl.multiple_of(zz * 2 * grp, 128), 2 * grp), :]
        lhs = jnp.concatenate([recv[zz * 2, side, at, :], recv[zz * 2 + 1, side, at, :]], axis=1)
        term = jnp.dot(lhs, xp, preferred_element_type=jnp.float32)
        cols_at = slice(side * rank, (side + 1) * rank)
        if k == 0:
            out_ref[at, cols_at] = term
        else:
            out_ref[at, cols_at] += term

    def take(k, zz):
        drain(recv.at[pl.ds(zz * 2, 2)], g_recv.at[zz])
        for side in (0, 1):
            add_term(k, zz, side, 0, rows)

    groups = xp_all.at[: 2 * grp, :]
    drain(groups, xc_recv.at[0])
    take(0, z)
    take(1, adj)
    drain(groups, xc_recv.at[1])
    for load in moments:
        load.wait()
    moved = (nt - 1) * nz + nt * nz + 2
    pl.when(inner == 0)(lambda: drain(xp_all.at[: moved * sub, :], xp_send.at[0]))
    pl.when(inner == 1)(lambda: drain(xp_all.at[: (moved + 2) * sub, :], xp_send.at[0]))
    take(2, far)

    @pl.when(inner == 0)
    def _():
        take(3, opp)

    @pl.when(inner == 1)
    def _():
        drain(recv.at[pl.ds(opp * 2, 2), 0], g_recv.at[opp])
        add_term(3, opp, 0, 0, rows)
        for p, (start, stop) in enumerate(cut):
            drain(recv.at[pl.ds(opp * 2, 2), 1, start:stop, :], cut_recv.at[p])
            add_term(3, opp, 1, start, stop - start)

    drain(recv.at[: ndp - 1], g_send.at[0])


def exchange(ndp, nt, tokens_in, projector, gate_pre, up_pre, hidden_grad, moment_m, moment_v):
    sub, width = tokens_in.shape
    depth, rank = projector.shape
    grp, cols = gate_pre.shape
    rows = cols // ndp
    dma = pltpu.SemaphoreType.DMA
    bf, f32 = jnp.bfloat16, jnp.float32
    nz = ndp // 2
    operands = (tokens_in, projector, gate_pre, up_pre, hidden_grad, moment_m, moment_v)
    flops = 2 * grp * depth * rank + 4 * rows * grp * ndp * rank
    return pl.pallas_call(
        functools.partial(exchange_kernel, ndp, nt),
        out_shape=(jax.ShapeDtypeStruct((rows, 2 * rank), f32),) * 3,
        in_specs=[pl.BlockSpec(memory_space=pltpu.HBM)] * 7,
        out_specs=(pl.BlockSpec(memory_space=pltpu.VMEM),) * 3,
        scratch_shapes=[
            pltpu.VMEM((3, grp, cols), bf),
            pltpu.VMEM((depth, rank), bf),
            pltpu.VMEM((grp, depth), bf),
            pltpu.VMEM((grp, rank), f32),
            pltpu.VMEM((nt, sub, rank), f32),
            pltpu.VMEM((grp * ndp, rank), bf),
            pltpu.VMEM((2, cols, grp), bf),
            pltpu.VMEM((ndp, 2, rows, grp), bf),
            dma((3,)),
            dma((1,)),
            dma((1,)),
            dma((1,)),
            dma((3,)),
            dma((2,)),
            dma((2,)),
            dma((1,)),
            dma((nz,)),
            dma((TAILS,)),
            pltpu.SemaphoreType.REGULAR,
            pltpu.SemaphoreType.REGULAR,
        ],
        compiler_params=pltpu.CompilerParams(
            collective_id=0, has_side_effects=True, vmem_limit_bytes=32 * 1024 * 1024
        ),
        cost_estimate=pl.CostEstimate(
            flops=flops, bytes_accessed=8 * grp * cols, transcendentals=grp * cols
        ),
    )(*[pltpu.with_memory_space_constraint(x, pltpu.HBM) for x in operands])


def fits(ndp, nt, tokens_in, projector, gate_pre):
    sub, width = tokens_in.shape
    grp, cols = gate_pre.shape
    return (
        ndp == 8
        and nt >= 2
        and grp == 128
        and sub * nt == grp
        and sub % 16 == 0
        and cols % ndp == 0
        and (cols // ndp) % 16 == 0
        and cols // ndp >= 256
        and cols % 256 == 0
        and width % (128 * nt) == 0
        and projector.shape[0] == width // nt
        and projector.shape[1] % 128 == 0
        and cols <= 8192
        and projector.size <= 2**21
        and grp * ndp <= 4096
    )


def finish(summed, total_tokens, moment_m, moment_v):
    proj = summed * float(total_tokens) ** (-0.5)
    m_next = 0.9 * moment_m + 0.1 * proj
    v_next = 0.95 * moment_v + 0.05 * proj * proj
    direction = m_next / (jnp.sqrt(v_next) + 1e-08)
    return (m_next, v_next, direction)


def finish_kernel(total_tokens, sum_ref, m_ref, v_ref, *refs):
    outs, bufs, sem = refs[:3], refs[3:6], refs[6]
    rows = sum_ref.shape[0]
    cuts = [0] + [-(-rows * k // 80) * 8 for k in (1, 2, 4, 6, 8)] + [rows]
    for at in map(slice, cuts, cuts[1:]):
        values = finish(sum_ref[at, :], total_tokens, m_ref[at, :], v_ref[at, :])
        for k in range(3):
            bufs[k][at, :] = values[k]
            copy = pltpu.make_async_copy(
                bufs[k].at[at, :], outs[k].at[at, :], sem.at[k]
            )
            copy.start()
    for k in range(3):
        pltpu.make_async_copy(bufs[k], outs[k], sem.at[k]).wait()


def finish_call(summed, moment_m, moment_v, total_tokens):
    shape = jax.ShapeDtypeStruct(summed.shape, jnp.float32)
    return pl.pallas_call(
        functools.partial(finish_kernel, total_tokens),
        out_shape=(shape,) * 3,
        in_specs=[pl.BlockSpec(memory_space=pltpu.VMEM)] * 3,
        out_specs=[pl.BlockSpec(memory_space=pltpu.HBM)] * 3,
        scratch_shapes=[pltpu.VMEM(summed.shape, jnp.float32)] * 3
        + [pltpu.SemaphoreType.DMA((3,))],
        compiler_params=pltpu.CompilerParams(vmem_limit_bytes=16 * 1024 * 1024),
    )(summed, moment_m, moment_v)


def local(tokens_in, projector, gate_pre, up_pre, hidden_grad, moment_m, moment_v):
    ndp, nt = lax.axis_size("dp"), lax.axis_size("tensor")
    if fits(ndp, nt, tokens_in, projector, gate_pre):
        operands = tokens_in, projector, gate_pre, up_pre, hidden_grad, moment_m, moment_v
        return tuple(finish_call(*exchange(ndp, nt, *operands), gate_pre.shape[0] * ndp))
    gate = gate_pre.astype(jnp.float32)
    hgrad = hidden_grad.astype(jnp.float32)
    sig = jax.nn.sigmoid(gate)
    upval = up_pre.astype(jnp.float32)
    grad_gate = (hgrad * upval * sig * (1.0 + gate * (1.0 - sig))).astype(jnp.bfloat16)
    grad_up = (hgrad * gate * sig).astype(jnp.bfloat16)
    grads = jnp.stack([grad_gate, grad_up])
    grads = lax.all_to_all(grads, "dp", split_axis=2, concat_axis=1, tiled=True)
    columns = lax.all_to_all(tokens_in, "tensor", split_axis=1, concat_axis=0, tiled=True)
    partial_xp = jnp.dot(columns, projector, preferred_element_type=jnp.float32)
    own_rows = lax.psum_scatter(partial_xp, "tensor", scatter_dimension=0, tiled=True).astype(
        jnp.bfloat16
    )
    xp = lax.all_gather(own_rows, ("dp", "tensor"), axis=0, tiled=True)
    contract = (((0,), (0,)), ((), ()))
    halves = [
        lax.dot_general(grads[k], xp, contract, preferred_element_type=jnp.float32) for k in (0, 1)
    ]
    summed = jnp.concatenate(halves, axis=1)
    return finish(summed, xp.shape[0], moment_m, moment_v)


def solution(mesh):
    return jax.shard_map(
        local,
        mesh=mesh,
        in_specs=(
            P(("dp", "tensor"), None),
            P("tensor", None),
            P("dp", "tensor"),
            P("dp", "tensor"),
            P("dp", "tensor"),
            P(("tensor", "dp"), None),
            P(("tensor", "dp"), None),
        ),
        out_specs=(P(("tensor", "dp"), None), P(("tensor", "dp"), None), P(("tensor", "dp"), None)),
        check_vma=False,
    )
```
